256 devices in a mesh: segment: 2 (over core), seq: 128 (over z, x, y).
Axes of the slice: x: 4, y: 4, z: 8, core: 2. Of those that a mesh axis runs over, the one named last changes fastest.
Arguments:
- tracks_in: bfloat16 [1, 128, 512, 1536], P(None, 'seq'), may hold values from -120 to 120
- w_qkv: bfloat16 [2, 1536, 2304], P('segment'), may hold values from -0.15625 to 0.15625
- w_out: bfloat16 [2, 768, 1536], P('segment'), may hold values from -0.21875 to 0.21875
- visible: int32 [1, 128, 512], P(None, 'seq'), may hold values 0 or 1
- neighbours: int32 [1, 8, 4, 2], replicated, may hold values from 0 to 3, as said below
Outputs:
- section_tokens: bfloat16 [2, 1, 128, 512, 1536], P('segment', None, 'seq')
The draws below stay inside these ranges and needn't reach their ends.
Inputs may be any that keep to these rules, and one draw needn't show every extreme that they name: `neighbours`: each row names 2 different track blocks, none of them the row's own block.
All inputs are finite; a program needn't handle non-finite values. No bound on the sum of `visible` on one device may be relied on, other than what follows from the above.
Results may differ from the reference program's by a relative error of at most 0.0042.
Values may be sent and summed in bfloat16 or wider, within the bound.
No kernel may reach another device: no remote copies, remote signals or barrier semaphores. Data moves between devices by JAX's collectives and lax.ppermute only.
A program may use at most 128 MiB of HBM per device.

```python
import math
import jax
import jax.numpy as jnp
from jax import lax

D = 1536
HEADS = 6
HDIM = 128
TRACKS = 512
BLOCK = 128
NB = 2
FRAMES = 16
MB = 1
VIDEOS = 8
GROUPS = 128
TRACK_DEV = 4
BLOCKS = 4
N_SEQ = 128


def draw_tracks_in(key, part):
    subkeys = jax.random.split(key, 3)
    feature_scale = jnp.exp(jax.random.uniform(subkeys[0], (D,), jnp.float32, -1.15, 1.15))
    row_scale = jnp.exp(jax.random.uniform(subkeys[1], (MB, GROUPS, TRACKS, 1), jnp.float32, -1.15, 1.15))
    values_base = jax.random.normal(subkeys[2], (MB, GROUPS, TRACKS, D), jnp.float32)
    return (values_base * row_scale * feature_scale).astype(jnp.bfloat16)


def draw_neighbours(key, part):
    draw_scores = jax.random.randint(key, (MB, VIDEOS, BLOCKS, BLOCKS - 1), 0, 1048576) * (BLOCKS - 1)
    draw_scores = draw_scores + jnp.arange(BLOCKS - 1, dtype=jnp.int32)
    ordering = jnp.argsort(draw_scores, axis=-1, stable=True)[..., :NB].astype(jnp.int32)
    own_block = jnp.arange(BLOCKS, dtype=jnp.int32).reshape(1, 1, BLOCKS, 1)
    return ((own_block + 1 + ordering) % BLOCKS).astype(jnp.int32)


def touch_ends(values, key, least, top_value):
    index_at = [jax.random.randint(jax.random.fold_in(key, axis), (), 0, length) for axis, length in enumerate(values.shape)]
    main_axis = values.shape.index(max(values.shape))
    next_to = index_at[:main_axis] + [(index_at[main_axis] + 1) % values.shape[main_axis]] + index_at[main_axis + 1:]
    return values.at[tuple(index_at)].set(least).at[tuple(next_to)].set(top_value)


def shard_levels(stream_key, shape, cuts, least, high):
    loudness = 1.0
    for dim, blocks in cuts:
        heights = jax.random.uniform(jax.random.fold_in(jax.random.fold_in(stream_key, 6), dim), (blocks,), jnp.float32, least / len(cuts), high / len(cuts))
        loudness = loudness * jnp.repeat(jnp.exp(heights), shape[dim] // blocks).reshape((-1,) + (1,) * (len(shape) - 1 - dim))
    return loudness


def scatter_about(rng, extent, scale, reach, pieces=(), held_as=jnp.bfloat16):
    level = shard_levels(rng, extent, pieces, -0.22, 0.18) if pieces else 1.0
    drawn = jax.random.normal(rng, extent, jnp.float32) * scale * level
    return jnp.minimum(jnp.maximum(drawn, -reach), reach).astype(held_as)


def setup_inputs(seed: int = 0) -> dict:
    arg_keys = jax.random.split(jax.random.key(seed), 6)
    tracks_in = draw_tracks_in(jax.random.fold_in(arg_keys[5], 71), 0)
    w_qkv = scatter_about(arg_keys[1], (2, D, 3 * HEADS * HDIM), D ** -0.5, 0.15625, ((0, 2),))
    w_out = scatter_about(arg_keys[2], (2, HEADS * HDIM, D), (HEADS * HDIM) ** -0.5, 0.21875, ((0, 2),))
    visible = touch_ends((jax.random.randint(arg_keys[3], (MB, GROUPS, TRACKS), 0, 4) < 3).astype(jnp.int32), jax.random.fold_in(arg_keys[3], 1), 0, 1)
    neighbours = draw_neighbours(jax.random.fold_in(arg_keys[5], 71), 0)
    return {"tracks_in": tracks_in, "w_qkv": w_qkv, "w_out": w_out, "visible": visible, "neighbours": neighbours}


epsilon = 1e-06

def normalize(tokens):
    widened = tokens.astype(jnp.float32)
    factor = lax.rsqrt(lax.optimization_barrier(jnp.mean(widened * widened, axis=-1, keepdims=True)) + epsilon)
    return (widened * factor).astype(jnp.bfloat16)

def project(tokens, weight):
    return jnp.dot(normalize(tokens), weight, preferred_element_type=jnp.float32).astype(jnp.bfloat16)

def finish(tokens, mixed_heads, weight):
    delta_rows = jnp.dot(mixed_heads, weight, preferred_element_type=jnp.float32)
    return (tokens.astype(jnp.float32) + delta_rows).astype(jnp.bfloat16)

def time_mix(projected):
    leading = projected.shape[:3]
    shaped = projected.astype(jnp.float32).reshape(leading + (3, HEADS, HDIM))
    queries = shaped[:, :, :, 0]
    keys_all = shaped[:, :, :, 1]
    values = shaped[:, :, :, 2]
    scores = jnp.einsum('vfphd,vgphd->vphfg', queries, keys_all) / math.sqrt(HDIM)
    exponent = jnp.exp(scores)
    weights = (exponent / lax.optimization_barrier(jnp.sum(exponent, axis=-1, keepdims=True))).astype(jnp.bfloat16)
    mixed_heads = jnp.einsum('vphfg,vgphd->vfphd', weights.astype(jnp.float32), values)
    return mixed_heads.reshape(leading + (HEADS * HDIM,)).astype(jnp.bfloat16)

def track_mix(projected, seen_mask, chosen):
    blocks_all = projected.astype(jnp.float32).reshape(BLOCKS, BLOCK, 3, HEADS, HDIM)
    own_block = lax.broadcasted_iota(jnp.int32, (BLOCKS, 1), 0)
    listing = jnp.concatenate([own_block, chosen.astype(jnp.int32)], axis=1)
    queries = blocks_all[:, :, 0]
    keys_sel = jnp.take(blocks_all[:, :, 1], listing, axis=0)
    values_sel = jnp.take(blocks_all[:, :, 2], listing, axis=0)
    seen_sel = jnp.take(seen_mask.reshape(BLOCKS, BLOCK), listing, axis=0)
    scores = jnp.einsum('bqhd,bjkhd->bhqjk', queries, keys_sel) / math.sqrt(HDIM)
    itself = (lax.broadcasted_iota(jnp.int32, (BLOCK, NB + 1, BLOCK), 1) == 0) & (lax.broadcasted_iota(jnp.int32, (BLOCK, NB + 1, BLOCK), 0) == lax.broadcasted_iota(jnp.int32, (BLOCK, NB + 1, BLOCK), 2))
    allowed = (seen_sel[:, None, None, :, :] == 1) | itself[None, None]
    exponent = jnp.where(allowed, jnp.exp(scores), jnp.zeros_like(scores))
    totals = lax.optimization_barrier(jnp.sum(exponent, axis=(-2, -1), keepdims=True))
    weights = (exponent / totals).astype(jnp.bfloat16)
    mixed_heads = jnp.einsum('bhqjk,bjkhd->bqhd', weights.astype(jnp.float32), values_sel)
    return mixed_heads.reshape(TRACKS, HEADS * HDIM).astype(jnp.bfloat16)

def reference(tracks_in, w_qkv, w_out, visible, neighbours):

    def one_batch(entries):
        tokens, seen_all, lists = entries
        flat_in = tokens.reshape(GROUPS * TRACKS, D)
        proj_first = project(flat_in, w_qkv[0]).reshape(VIDEOS, FRAMES, TRACKS, 3 * HEADS * HDIM)
        mixed_first = time_mix(proj_first).reshape(GROUPS * TRACKS, HEADS * HDIM)
        first = finish(flat_in, mixed_first, w_out[0])
        proj_second = project(first, w_qkv[1]).reshape(GROUPS, TRACKS, 3 * HEADS * HDIM)
        group_lists = jnp.repeat(lists, FRAMES, axis=0)
        mixed_second = lax.map(lambda parts: track_mix(parts[0], parts[1], parts[2]), (proj_second, seen_all, group_lists))
        second = finish(first, mixed_second.reshape(GROUPS * TRACKS, HEADS * HDIM), w_out[1])
        regrouped = first.reshape(GROUPS, N_SEQ, TRACK_DEV, D).transpose(1, 0, 2, 3).reshape(N_SEQ, GROUPS * TRACK_DEV, D)
        return (regrouped, second.reshape(GROUPS, TRACKS, D))
    firsts, seconds = lax.map(one_batch, (tracks_in, visible, neighbours))
    return jnp.stack([firsts, seconds])
```

```python
import math

import jax
import jax.numpy as jnp
from jax import lax
from jax.experimental import pallas as pl
from jax.experimental.pallas import tpu as pltpu
from jax.sharding import Mesh, PartitionSpec as P

HEADS = 6
HDIM = 128
BLOCK = 128
FRAMES = 16
INNER = HEADS * HDIM
PAIR = 2 * HDIM
PAIRS = HEADS // 2
EPS = 1e-06
SCALE = 1.0 / math.sqrt(HDIM)

f32 = jnp.float32
bf16 = jnp.bfloat16


def regroup(rows, outer, inner, unit):
    to = lax.broadcasted_iota(jnp.int32, (rows, rows), 0)
    source = lax.broadcasted_iota(jnp.int32, (rows, rows), 1)
    u = to % unit
    o = (to // unit) % outer
    i = to // (unit * outer)
    return (source == o * (inner * unit) + i * unit + u).astype(bf16)


def permute_rows(one_hot, value):
    return jnp.dot(one_hot, value, preferred_element_type=f32).astype(bf16)


def spread_kernel(x_ref, p_ref, o_ref):
    o_ref[...] = permute_rows(p_ref[...], x_ref[...])


def spread(x, one_hot, columns=512):
    rows, width = x.shape
    return pl.pallas_call(
        spread_kernel,
        out_shape=jax.ShapeDtypeStruct((rows, width), bf16),
        grid=(width // columns,),
        in_specs=[
            pl.BlockSpec((rows, columns), lambda j: (0, j)),
            pl.BlockSpec((rows, rows), lambda j: (0, 0)),
        ],
        out_specs=pl.BlockSpec((rows, columns), lambda j: (0, j)),
        name="spread",
    )(x, one_hot)


def row_factor(x):
    wide = x.astype(f32)
    return lax.rsqrt(jnp.mean(wide * wide, axis=-1, keepdims=True) + EPS)


def load_qkv(w_hbm, w_buf, sem):
    copies = []
    for pair in range(PAIRS):
        for part in range(3):
            columns = pl.ds(part * INNER + pair * PAIR, PAIR)
            copies.append(
                pltpu.make_async_copy(
                    w_hbm.at[:, columns], w_buf.at[:, columns], sem.at[pair, part]
                )
            )
    for copy in copies:
        copy.start()
    return copies


def time_kernel(x_ref, w_hbm, o_ref, w_buf, sem):
    copies = load_qkv(w_hbm, w_buf, sem)
    rows = x_ref.shape[0]
    tracks = rows // FRAMES
    x = x_ref[...]
    factor = row_factor(x)
    side = FRAMES * 8
    same = (
        lax.broadcasted_iota(jnp.int32, (side, side), 0) % 8
        == lax.broadcasted_iota(jnp.int32, (side, side), 1) % 8
    )
    for pair in range(PAIRS):
        parts = []
        for part in range(3):
            copies[pair * 3 + part].wait()
            columns = pl.ds(part * INNER + pair * PAIR, PAIR)
            y = jnp.dot(x, w_buf[:, columns], preferred_element_type=f32) * factor
            parts.append(y.reshape(FRAMES, tracks, PAIR))
        for head in range(2):
            for group in range(tracks // 8):
                q, k, v = (
                    y[:, group * 8 : group * 8 + 8, head * HDIM : head * HDIM + HDIM]
                    .reshape(side, HDIM)
                    .astype(bf16)
                    for y in parts
                )
                scores = lax.dot_general(
                    q, k, (((1,), (1,)), ((), ())), preferred_element_type=f32
                )
                e = jnp.where(same, jnp.exp(scores * SCALE), 0.0)
                weights = (e / jnp.sum(e, axis=-1, keepdims=True)).astype(bf16)
                mixed = jnp.dot(weights, v, preferred_element_type=f32)
                at = (pair * 2 + head) * HDIM
                o_ref[:, group * 8 : group * 8 + 8, at : at + HDIM] = mixed.reshape(
                    FRAMES, 8, HDIM
                ).astype(bf16)


def time_section(x, w):
    rows, width = x.shape
    return pl.pallas_call(
        time_kernel,
        out_shape=jax.ShapeDtypeStruct((FRAMES, rows // FRAMES, INNER), bf16),
        in_specs=[
            pl.BlockSpec(memory_space=pltpu.VMEM),
            pl.BlockSpec(memory_space=pl.ANY),
        ],
        out_specs=pl.BlockSpec(memory_space=pltpu.VMEM),
        scratch_shapes=[
            pltpu.VMEM((width, 3 * INNER), bf16),
            pltpu.SemaphoreType.DMA((PAIRS, 3)),
        ],
        compiler_params=pltpu.CompilerParams(vmem_limit_bytes=40 << 20),
        name="time_section",
    )(x, w)


def finish_kernel(x_ref, m_ref, w_ref, p_ref, o_ref):
    delta = jnp.dot(m_ref[...], w_ref[...], preferred_element_type=f32)
    first = (x_ref[...].astype(f32) + delta).astype(bf16)
    o_ref[...] = permute_rows(p_ref[...], first)


def finish_first(x, mixed, w, one_hot, columns=512):
    rows, width = x.shape
    return pl.pallas_call(
        finish_kernel,
        out_shape=jax.ShapeDtypeStruct((rows, width), bf16),
        grid=(width // columns,),
        in_specs=[
            pl.BlockSpec((rows, columns), lambda j: (0, j)),
            pl.BlockSpec((rows, INNER), lambda j: (0, 0)),
            pl.BlockSpec((INNER, columns), lambda j: (0, j)),
            pl.BlockSpec((rows, rows), lambda j: (0, 0)),
        ],
        out_specs=pl.BlockSpec((rows, columns), lambda j: (0, j)),
        name="finish_first",
    )(x, mixed, w, one_hot)


def track_kernel(
    lists, x_ref, m_ref, p_ref, seen_ref, w0_hbm, wq_hbm, w1_hbm, o_ref,
    w0, wq, w1, first, qkv, mixed1, sem, sem_out,
):
    copy_0 = pltpu.make_async_copy(w0_hbm, w0, sem_out.at[0])
    copy_0.start()
    copies = load_qkv(wq_hbm, wq, sem)
    copy_1 = pltpu.make_async_copy(w1_hbm, w1, sem_out.at[1])
    copy_1.start()
    rows = x_ref.shape[0]
    blocks = rows // BLOCK
    mixed0 = permute_rows(p_ref[...], m_ref[...])
    copy_0.wait()
    delta = jnp.dot(mixed0, w0[...], preferred_element_type=f32)
    first[...] = (x_ref[...].astype(f32) + delta).astype(bf16)
    factor = row_factor(first[...])
    itself = lax.broadcasted_iota(jnp.int32, (BLOCK, BLOCK), 0) == lax.broadcasted_iota(
        jnp.int32, (BLOCK, BLOCK), 1
    )
    for pair in range(PAIRS):
        for part in range(3):
            copies[pair * 3 + part].wait()
            columns = pl.ds(part * INNER + pair * PAIR, PAIR)
            y = jnp.dot(first[...], wq[:, columns], preferred_element_type=f32) * factor
            qkv[:, columns] = y.astype(bf16)
        for block in range(blocks):
            others = [lists[block * 2], lists[block * 2 + 1]]
            places = [pl.ds(block * BLOCK, BLOCK)] + [
                pl.ds(pl.multiple_of(o * BLOCK, BLOCK), BLOCK) for o in others
            ]
            allowed = [(seen_ref[block : block + 1, :] == 1) | itself] + [
                seen_ref[pl.ds(o, 1), :] == 1 for o in others
            ]
            for head in range(2):
                at = (pair * 2 + head) * HDIM
                q = qkv[pl.ds(block * BLOCK, BLOCK), at : at + HDIM]
                es = []
                for place, allow in zip(places, allowed):
                    k = qkv[place, INNER + at : INNER + at + HDIM]
                    scores = lax.dot_general(
                        q, k, (((1,), (1,)), ((), ())), preferred_element_type=f32
                    )
                    es.append(jnp.where(allow, jnp.exp(scores * SCALE), 0.0))
                total = sum(jnp.sum(e, axis=-1, keepdims=True) for e in es)
                acc = None
                for place, e in zip(places, es):
                    v = qkv[place, 2 * INNER + at : 2 * INNER + at + HDIM]
                    part_sum = jnp.dot((e / total).astype(bf16), v, preferred_element_type=f32)
                    acc = part_sum if acc is None else acc + part_sum
                mixed1[pl.ds(block * BLOCK, BLOCK), at : at + HDIM] = acc.astype(bf16)
    copy_1.wait()
    delta = jnp.dot(mixed1[...], w1[...], preferred_element_type=f32)
    o_ref[...] = (first[...].astype(f32) + delta).astype(bf16)


def track_section(lists, x, mixed0, one_hot, seen, w_out0, w_qkv, w_out1):
    rows, width = x.shape
    vmem = pl.BlockSpec(memory_space=pltpu.VMEM)
    hbm = pl.BlockSpec(memory_space=pl.ANY)
    return pl.pallas_call(
        track_kernel,
        out_shape=jax.ShapeDtypeStruct((rows, width), bf16),
        in_specs=[pl.BlockSpec(memory_space=pltpu.SMEM), vmem, vmem, vmem, vmem, hbm, hbm, hbm],
        out_specs=vmem,
        scratch_shapes=[
            pltpu.VMEM((INNER, width), bf16),
            pltpu.VMEM((width, 3 * INNER), bf16),
            pltpu.VMEM((INNER, width), bf16),
            pltpu.VMEM((rows, width), bf16),
            pltpu.VMEM((rows, 3 * INNER), bf16),
            pltpu.VMEM((rows, INNER), bf16),
            pltpu.SemaphoreType.DMA((PAIRS, 3)),
            pltpu.SemaphoreType.DMA((2,)),
        ],
        compiler_params=pltpu.CompilerParams(vmem_limit_bytes=48 << 20),
        name="track_section",
    )(lists, x, mixed0, one_hot, seen, w_out0, w_qkv, w_out1)


def exchange(value, axis):
    return lax.all_to_all(value, axis, split_axis=0, concat_axis=0, tiled=True)


def on_device(tracks_in, w_qkv, w_out, visible, neighbours):
    segment_no = lax.axis_index("segment")
    video_no = lax.axis_index("z")
    planes = lax.axis_size("z")
    frames = lax.axis_size("plane")
    x = tracks_in[0, 0]
    rows, width = x.shape
    per_chip = rows // frames
    unit = per_chip // planes
    w_in, w_back = w_qkv[0], w_out[0]
    seen = visible[0, 0].reshape(rows // BLOCK, BLOCK)
    lists = lax.dynamic_index_in_dim(neighbours[0], video_no, 0, keepdims=False).reshape(-1)
    to_chips = regroup(rows, planes, frames, unit)
    to_tracks = regroup(rows, frames, planes, unit)
    w_back_first = lax.ppermute(w_back, "segment", [(0, 1)])

    def section_one():
        sent = spread(x, to_chips).reshape(frames, per_chip, width)
        moved = exchange(sent, "plane").reshape(rows, width)
        return moved, time_section(moved, w_in)

    def idle():
        return jnp.zeros((rows, width), bf16), jnp.zeros((frames, per_chip, INNER), bf16)

    moved, mixed0 = lax.cond(segment_no == 0, section_one, idle)
    handed = lax.ppermute(mixed0, "segment", [(0, 1)])

    def track_order():
        first = finish_first(moved, mixed0.reshape(rows, INNER), w_back, to_tracks)
        return exchange(first.reshape(planes, frames * unit, width), "z").reshape(rows, width)

    def section_two():
        back = exchange(handed, "plane").reshape(rows, INNER)
        return track_section(lists, x, back, to_tracks, seen, w_back_first, w_in, w_back)

    result = lax.cond(segment_no == 0, track_order, section_two)
    return result[None, None, None]


def solution(mesh):
    frames = FRAMES
    devices = mesh.devices.reshape(mesh.devices.shape[0], -1, frames)
    grid = Mesh(devices, ("segment", "z", "plane"))
    seq = ("z", "plane")
    return jax.shard_map(
        on_device,
        mesh=grid,
        in_specs=(
            P(None, seq, None, None),
            P("segment", None, None),
            P("segment", None, None),
            P(None, seq, None),
            P(),
        ),
        out_specs=P("segment", None, seq, None, None),
        check_vma=False,
    )
```

```python
import functools
import math

import jax
import jax.numpy as jnp
from jax import lax
from jax.experimental import pallas as pl
from jax.experimental.pallas import tpu as pltpu
from jax.sharding import Mesh, PartitionSpec as P

HEADS = 6
HDIM = 128
BLOCK = 128
FRAMES = 16
UNIT = 4
INNER = HEADS * HDIM
PAIR = 2 * HDIM
PAIRS = HEADS // 2
EPS = 1e-06
SCALE = math.log2(math.e) / math.sqrt(HDIM)
LOW = -1e30

f32 = jnp.float32
bf16 = jnp.bfloat16


def regroup(value, outer, inner, store):
    width = value.shape[-1]
    grouped = value.reshape(outer // 2, 2, inner // 2, 8, width)
    low = lax.broadcasted_iota(jnp.int32, (8, width), 0) < 4
    for a in range(inner // 2):
        evens = [grouped[c, 0, a] for c in range(outer // 2)]
        odds = [grouped[c, 1, a] for c in range(outer // 2)]
        lower = [jnp.where(low, e, pltpu.roll(o, 4, 0)) for e, o in zip(evens, odds)]
        upper = [jnp.where(low, pltpu.roll(e, 4, 0), o) for e, o in zip(evens, odds)]
        store(a * 2 * outer * 4, jnp.concatenate(lower + upper, axis=0))


def regroup_into(o_ref, value, outer, inner):
    def store(at, rows):
        o_ref[at : at + rows.shape[0], :] = rows.astype(o_ref.dtype)

    regroup(value, outer, inner, store)


def spread_kernel(half, x_ref, o_ref):
    outer, each, width = x_ref.shape
    value = x_ref[...].astype(f32).reshape(outer * each, width)
    regroup_into(o_ref, value, outer, each // UNIT)


def spread(x, half, planes, steps=1):
    rows, width = x.shape
    each = rows // planes
    outer = planes // 2
    grid_spec = pltpu.PrefetchScalarGridSpec(
        num_scalar_prefetch=1,
        grid=(steps,),
        in_specs=[pl.BlockSpec((outer, each // steps, width), lambda j, half: (half[0], j, 0))],
        out_specs=pl.BlockSpec((rows // 2 // steps, width), lambda j, half: (j, 0)),
    )
    return pl.pallas_call(
        spread_kernel,
        out_shape=jax.ShapeDtypeStruct((rows // 2, width), bf16),
        grid_spec=grid_spec,
        name="spread",
    )(half, x.reshape(planes, each, width))


def row_factor(x):
    wide = x.astype(f32)
    return lax.rsqrt(jnp.mean(wide * wide, axis=-1, keepdims=True) + EPS)


def similar(q, k):
    return lax.dot_general(q, k, (((1,), (1,)), ((), ())), preferred_element_type=f32)


def time_kernel(
    half, x_hbm, own_hbm, sent_hbm, back_own, back_sent, first_hbm, mixed_hbm, given_hbm,
    x_buf, w, w_back, mixed, first, sem, sem_w,
):
    rows, width = x_buf.shape
    tracks = rows // FRAMES
    groups = tracks // 8
    side = FRAMES * 8
    get_x = pltpu.make_async_copy(x_hbm, x_buf, sem.at[0])

    def gets(source):
        return [
            pltpu.make_async_copy(
                source.at[:, pl.ds(part * INNER + pair * PAIR, PAIR)],
                w.at[:, pl.ds(part * INNER + pair * PAIR, PAIR)],
                sem_w.at[pair * 3 + part],
            )
            for pair in range(PAIRS)
            for part in range(3)
        ]

    get_back = pltpu.make_async_copy(back_own, w_back, sem.at[2])
    get_x.start()

    @pl.when(half[0] == 0)
    def _():
        for get in gets(own_hbm):
            get.start()
        get_back.start()

    @pl.when(half[0] != 0)
    def _():
        for get in gets(sent_hbm):
            get.start()
        pltpu.make_async_copy(back_sent, w_back, sem.at[2]).start()

    same = (
        lax.broadcasted_iota(jnp.int32, (side, side), 0) % 8
        == lax.broadcasted_iota(jnp.int32, (side, side), 1) % 8
    )
    get_x.wait()
    x = x_buf[...]
    factor = row_factor(x)
    get_w = gets(own_hbm)
    for pair in range(PAIRS):
        parts = []
        for get in get_w[pair * 3 : pair * 3 + 3]:
            get.wait()
        for part in range(3):
            at = part * INNER + pair * PAIR
            y = jnp.dot(x, w[:, at : at + PAIR], preferred_element_type=f32) * factor
            parts.append(y.reshape(FRAMES, tracks, PAIR))
        places = [(head, group) for head in range(2) for group in range(groups)]
        blocks = [
            [
                y[:, group * 8 : group * 8 + 8, head * HDIM : head * HDIM + HDIM]
                .reshape(side, HDIM)
                .astype(bf16)
                for y in parts
            ]
            for head, group in places
        ]
        scores = [jnp.where(same, similar(q, k), LOW) for q, k, v in blocks]
        tops = [jnp.max(s, axis=-1, keepdims=True) for s in scores]
        es = [jnp.exp2((s - top) * SCALE) for s, top in zip(scores, tops)]
        totals = [jnp.sum(e, axis=-1, keepdims=True) for e in es]
        sums = [
            jnp.dot(e.astype(bf16), v, preferred_element_type=f32) for e, (q, k, v) in zip(es, blocks)
        ]
        for (head, group), total, summed in zip(places, totals, sums):
            at = (pair * 2 + head) * HDIM
            mixed[:, group * 8 : group * 8 + 8, at : at + HDIM] = (
                (summed * (1.0 / total)).reshape(FRAMES, 8, HDIM).astype(bf16)
            )
    m = mixed[...].reshape(rows, INNER)
    get_back.wait()
    delta = jnp.dot(m, w_back[...], preferred_element_type=f32)
    regroup_into(first, x.astype(f32) + delta, FRAMES, tracks // UNIT)

    @pl.when(half[0] == 0)
    def _():
        puts = [
            pltpu.make_async_copy(mixed, given_hbm.at[:, :, :INNER], sem.at[3]),
            pltpu.make_async_copy(first, first_hbm.at[pl.ds(0, rows), :], sem.at[4]),
        ]
        for put in puts:
            put.start()
        for put in puts:
            put.wait()

    @pl.when(half[0] != 0)
    def _():
        puts = [
            pltpu.make_async_copy(first, given_hbm.reshape(rows, width), sem.at[3]),
            pltpu.make_async_copy(mixed, mixed_hbm.at[:, pl.ds(tracks, tracks), :], sem.at[4]),
        ]
        for put in puts:
            put.start()
        for put in puts:
            put.wait()


def time_section(half, x, w_own, w_sent, back_own, back_sent):
    rows, width = x.shape
    tracks = rows // FRAMES
    hbm = pl.BlockSpec(memory_space=pl.ANY)
    return pl.pallas_call(
        time_kernel,
        out_shape=[
            jax.ShapeDtypeStruct((2 * rows, width), bf16),
            jax.ShapeDtypeStruct((FRAMES, 2 * tracks, INNER), bf16),
            jax.ShapeDtypeStruct((FRAMES, tracks, width), bf16),
        ],
        in_specs=[pl.BlockSpec(memory_space=pltpu.SMEM)] + [hbm] * 5,
        out_specs=[hbm] * 3,
        scratch_shapes=[
            pltpu.VMEM((rows, width), bf16),
            pltpu.VMEM((width, 3 * INNER), bf16),
            pltpu.VMEM((INNER, width), bf16),
            pltpu.VMEM((FRAMES, tracks, INNER), bf16),
            pltpu.VMEM((rows, width), bf16),
            pltpu.SemaphoreType.DMA((5,)),
            pltpu.SemaphoreType.DMA((3 * PAIRS,)),
        ],
        compiler_params=pltpu.CompilerParams(vmem_limit_bytes=32 << 20),
        name="time_section",
    )(half, x, w_own, w_sent, back_own, back_sent)


def join_kernel(place, columns, part_ref, whole_hbm, o_hbm, sem):
    del whole_hbm
    put = pltpu.make_async_copy(part_ref.at[columns], o_hbm.at[place], sem)
    put.start()
    put.wait()


def join(part, whole, place, columns):
    hbm = pl.BlockSpec(memory_space=pl.ANY)
    return pl.pallas_call(
        functools.partial(join_kernel, place, columns),
        out_shape=jax.ShapeDtypeStruct(whole.shape, whole.dtype),
        in_specs=[pl.BlockSpec(memory_space=pltpu.VMEM), hbm],
        out_specs=hbm,
        scratch_shapes=[pltpu.SemaphoreType.DMA],
        input_output_aliases={1: 0},
        compiler_params=pltpu.CompilerParams(vmem_limit_bytes=4 << 20),
        name="join",
    )(part, whole)


def track_kernel(
    planes, lists, m_ref, seen_ref, x_hbm, w0_hbm, wq_hbm, w1_hbm, o_ref,
    x_buf, w0, wq, w1, mixed0, first, qkv_0, qkv_1, qkv_2, mixed1, sem_more,
):
    rows = x_buf.shape[0]
    blocks = rows // BLOCK
    get_w0 = pltpu.make_async_copy(w0_hbm, w0, sem_more.at[0])
    get_x = pltpu.make_async_copy(x_hbm, x_buf, sem_more.at[1])
    get_w1 = pltpu.make_async_copy(w1_hbm, w1, sem_more.at[2])
    get_wq = pltpu.make_async_copy(wq_hbm, wq, sem_more.at[3])
    for copy in (get_w0, get_x, get_wq, get_w1):
        copy.start()
    regroup_into(mixed0, m_ref[...].astype(f32), FRAMES, planes)
    get_w0.wait()
    delta = jnp.dot(mixed0[...], w0[...], preferred_element_type=f32)
    get_x.wait()
    first[...] = (x_buf[...].astype(f32) + delta).astype(bf16)
    factor = row_factor(first[...])
    itself = lax.broadcasted_iota(jnp.int32, (BLOCK, BLOCK), 0) == lax.broadcasted_iota(
        jnp.int32, (BLOCK, BLOCK), 1
    )
    get_wq.wait()
    for pair, qkv in enumerate((qkv_0, qkv_1, qkv_2)):
        for part in range(3):
            at = part * INNER + pair * PAIR
            y = jnp.dot(first[...], wq[:, at : at + PAIR], preferred_element_type=f32) * factor
            qkv[:, part * PAIR : (part + 1) * PAIR] = y.astype(bf16)
        for head in range(2):
            at = head * HDIM
            out_at = (pair * 2 + head) * HDIM
            groups = []
            for block in range(blocks):
                others = [lists[block * 2], lists[block * 2 + 1]]
                places = [pl.ds(block * BLOCK, BLOCK)] + [
                    pl.ds(pl.multiple_of(o * BLOCK, BLOCK), BLOCK) for o in others
                ]
                allowed = [(seen_ref[block : block + 1, :] == 1) | itself] + [
                    seen_ref[pl.ds(o, 1), :] == 1 for o in others
                ]
                q = qkv[pl.ds(block * BLOCK, BLOCK), at : at + HDIM]
                groups.append((q, places, allowed))
            scores = [
                [
                    jnp.where(allow, similar(q, qkv[place, PAIR + at : PAIR + at + HDIM]), LOW)
                    for place, allow in zip(places, allowed)
                ]
                for q, places, allowed in groups
            ]
            tops = [
                jnp.max(functools.reduce(jnp.maximum, ss), axis=-1, keepdims=True) for ss in scores
            ]
            es = [[jnp.exp2((s - top) * SCALE) for s in ss] for ss, top in zip(scores, tops)]
            totals = [jnp.sum(sum(e[1:], e[0]), axis=-1, keepdims=True) for e in es]
            sums = [
                sum(
                    jnp.dot(
                        e.astype(bf16),
                        qkv[place, 2 * PAIR + at : 2 * PAIR + at + HDIM],
                        preferred_element_type=f32,
                    )
                    for e, place in zip(parts, places)
                )
                for parts, (q, places, allowed) in zip(es, groups)
            ]
            for block, (total, mixed) in enumerate(zip(totals, sums)):
                mixed1[block * BLOCK : (block + 1) * BLOCK, out_at : out_at + HDIM] = (
                    mixed * (1.0 / total)
                ).astype(bf16)
    get_w1.wait()
    delta = jnp.dot(mixed1[...], w1[...], preferred_element_type=f32)
    o_ref[...] = (first[...].astype(f32) + delta).astype(bf16)


def track_section(lists, x, mixed0, seen, w_out0, w_qkv, w_out1, planes):
    rows, width = x.shape
    vmem = pl.BlockSpec(memory_space=pltpu.VMEM)
    return pl.pallas_call(
        functools.partial(track_kernel, planes),
        out_shape=jax.ShapeDtypeStruct((rows, width), bf16),
        in_specs=[pl.BlockSpec(memory_space=pltpu.SMEM), vmem, vmem]
        + [pl.BlockSpec(memory_space=pl.ANY)] * 4,
        out_specs=vmem,
        scratch_shapes=[
            pltpu.VMEM((rows, width), bf16),
            pltpu.VMEM((INNER, width), bf16),
            pltpu.VMEM((width, 3 * INNER), bf16),
            pltpu.VMEM((INNER, width), bf16),
            pltpu.VMEM((rows, INNER), bf16),
            pltpu.VMEM((rows, width), bf16),
            pltpu.VMEM((rows, 3 * PAIR), bf16),
            pltpu.VMEM((rows, 3 * PAIR), bf16),
            pltpu.VMEM((rows, 3 * PAIR), bf16),
            pltpu.VMEM((rows, INNER), bf16),
            pltpu.SemaphoreType.DMA((4,)),
        ],
        compiler_params=pltpu.CompilerParams(vmem_limit_bytes=40 << 20),
        name="track_section",
    )(lists, mixed0, seen, x, w_out0, w_qkv, w_out1)


def exchange(value, axis):
    return lax.all_to_all(value, axis, split_axis=0, concat_axis=0, tiled=True)


def on_device(tracks_in, w_qkv, w_out, visible, neighbours):
    segment_no = lax.axis_index("segment")
    video_no = lax.axis_index("z")
    planes = lax.axis_size("z")
    frames = lax.axis_size("plane")
    x = tracks_in[0, 0]
    rows, width = x.shape
    per_chip = rows // frames
    w_in, w_back = w_qkv[0], w_out[0]
    seen = visible[0, 0].reshape(rows // BLOCK, BLOCK)
    lists = lax.dynamic_index_in_dim(neighbours[0], video_no, 0, keepdims=False).reshape(-1)
    half = segment_no.reshape(1).astype(jnp.int32)
    sent = spread(x, half, planes).reshape(frames, per_chip // 2, width)
    sent, w_in_sent, w_back_sent = lax.optimization_barrier((sent, w_in, w_back))
    moved = exchange(sent, "plane").reshape(rows // 2, width)
    w_in_first = lax.ppermute(w_in_sent, "segment", [(0, 1)])
    w_back_first = lax.ppermute(w_back_sent, "segment", [(0, 1)])
    first, mixed0, given = time_section(half, moved, w_in, w_in_first, w_back, w_back_first)
    taken = lax.ppermute(given, "segment", [(0, 1), (1, 0)])
    each = per_chip // 2

    def track_order():
        other = taken.reshape(rows // 2, width)
        whole = join(other, first, (pl.ds(rows // 2, rows // 2),), (pl.ds(0, rows // 2),))
        return exchange(whole.reshape(planes, -1, width), "z").reshape(rows, width)

    def section_two():
        everything = slice(None)
        place = (everything, pl.ds(0, each), everything)
        whole = join(taken, mixed0, place, (everything, everything, pl.ds(0, INNER)))
        back = exchange(whole, "plane").reshape(rows, INNER)
        return track_section(lists, x, back, seen, w_back_first, w_in, w_back, planes)

    result = lax.cond(segment_no == 0, track_order, section_two)
    return result[None, None, None]


def solution(mesh):
    frames = FRAMES
    devices = mesh.devices.reshape(mesh.devices.shape[0], -1, frames)
    grid = Mesh(devices, ("segment", "z", "plane"))
    seq = ("z", "plane")
    return jax.shard_map(
        on_device,
        mesh=grid,
        in_specs=(
            P(None, seq, None, None),
            P("segment", None, None),
            P("segment", None, None),
            P(None, seq, None),
            P(),
        ),
        out_specs=P("segment", None, seq, None, None),
        check_vma=False,
    )
```

```python
import functools
import math

import jax
import jax.numpy as jnp
from jax import lax
from jax.experimental import pallas as pl
from jax.experimental.pallas import tpu as pltpu
from jax.sharding import Mesh, PartitionSpec as P

HEADS = 6
HDIM = 128
BLOCK = 128
FRAMES = 16
UNIT = 4
INNER = HEADS * HDIM
PAIR = 2 * HDIM
PAIRS = HEADS // 2
EPS = 1e-06
SCALE = math.log2(math.e) / math.sqrt(HDIM)
LOW = -1e30

f32 = jnp.float32
bf16 = jnp.bfloat16


def regroup(value, outer, inner, store):
    width = value.shape[-1]
    grouped = value.reshape(outer // 2, 2, inner // 2, 8, width)
    low = lax.broadcasted_iota(jnp.int32, (8, width), 0) < 4
    for a in range(inner // 2):
        evens = [grouped[c, 0, a] for c in range(outer // 2)]
        odds = [grouped[c, 1, a] for c in range(outer // 2)]
        lower = [jnp.where(low, e, pltpu.roll(o, 4, 0)) for e, o in zip(evens, odds)]
        upper = [jnp.where(low, pltpu.roll(e, 4, 0), o) for e, o in zip(evens, odds)]
        store(a * 2 * outer * 4, jnp.concatenate(lower + upper, axis=0))


def regroup_into(o_ref, value, outer, inner):
    def store(at, rows):
        o_ref[at : at + rows.shape[0], :] = rows.astype(o_ref.dtype)

    regroup(value, outer, inner, store)


def spread_kernel(half, x_ref, o_ref):
    outer, each, width = x_ref.shape
    value = x_ref[...].astype(f32).reshape(outer * each, width)
    regroup_into(o_ref, value, outer, each // UNIT)


def spread(x, half, planes, steps=1):
    rows, width = x.shape
    each = rows // planes
    outer = planes // 2
    grid_spec = pltpu.PrefetchScalarGridSpec(
        num_scalar_prefetch=1,
        grid=(steps,),
        in_specs=[pl.BlockSpec((outer, each // steps, width), lambda j, half: (half[0], j, 0))],
        out_specs=pl.BlockSpec((rows // 2 // steps, width), lambda j, half: (j, 0)),
    )
    return pl.pallas_call(
        spread_kernel,
        out_shape=jax.ShapeDtypeStruct((rows // 2, width), bf16),
        grid_spec=grid_spec,
        name="spread",
    )(half, x.reshape(planes, each, width))


def row_factor(x):
    wide = x.astype(f32)
    return lax.rsqrt(jnp.mean(wide * wide, axis=-1, keepdims=True) + EPS)


def similar(q, k):
    return lax.dot_general(q, k, (((1,), (1,)), ((), ())), preferred_element_type=f32)


def qkv_copies(source, target, sem):
    copies = []
    for pair in range(PAIRS):
        for part in range(3):
            columns = pl.ds(part * INNER + pair * PAIR, PAIR)
            copies.append(
                pltpu.make_async_copy(
                    source.at[:, columns], target.at[:, columns], sem.at[pair * 3 + part]
                )
            )
    return copies


def time_kernel(
    half, x_buf, own_hbm, sent_hbm, back_own, back_sent, first_ref, mixed_hbm, given_ref,
    w, w_back, mixed, sem, sem_w, sem_out,
):
    rows, width = x_buf.shape
    tracks = rows // FRAMES
    groups = tracks // 8
    side = FRAMES * 8
    get_back = pltpu.make_async_copy(back_own, w_back, sem)

    @pl.when(half[0] == 0)
    def _():
        for get in qkv_copies(own_hbm, w, sem_w):
            get.start()
        get_back.start()

    @pl.when(half[0] != 0)
    def _():
        for get in qkv_copies(sent_hbm, w, sem_w):
            get.start()
        pltpu.make_async_copy(back_sent, w_back, sem).start()

    same = (
        lax.broadcasted_iota(jnp.int32, (side, side), 0) % 8
        == lax.broadcasted_iota(jnp.int32, (side, side), 1) % 8
    )
    x = x_buf[...]
    factor = row_factor(x)
    get_w = qkv_copies(own_hbm, w, sem_w)
    for pair in range(PAIRS):
        parts = []
        for get in get_w[pair * 3 : pair * 3 + 3]:
            get.wait()
        for part in range(3):
            at = part * INNER + pair * PAIR
            y = jnp.dot(x, w[:, at : at + PAIR], preferred_element_type=f32) * factor
            parts.append(y.reshape(FRAMES, tracks, PAIR))
        places = [(head, group) for head in range(2) for group in range(groups)]
        blocks = [
            [
                y[:, group * 8 : group * 8 + 8, head * HDIM : head * HDIM + HDIM]
                .reshape(side, HDIM)
                .astype(bf16)
                for y in parts
            ]
            for head, group in places
        ]
        scores = [jnp.where(same, similar(q, k), LOW) for q, k, v in blocks]
        tops = [jnp.max(s, axis=-1, keepdims=True) for s in scores]
        es = [jnp.exp2((s - top) * SCALE) for s, top in zip(scores, tops)]
        totals = [jnp.sum(e, axis=-1, keepdims=True) for e in es]
        sums = [
            jnp.dot(e.astype(bf16), v, preferred_element_type=f32) for e, (q, k, v) in zip(es, blocks)
        ]
        for (head, group), total, summed in zip(places, totals, sums):
            at = (pair * 2 + head) * HDIM
            mixed[:, group * 8 : group * 8 + 8, at : at + HDIM] = (
                (summed * (1.0 / total)).reshape(FRAMES, 8, HDIM).astype(bf16)
            )
    m = mixed[...].reshape(rows, INNER)
    get_back.wait()
    delta = jnp.dot(m, w_back[...], preferred_element_type=f32)
    first = x.astype(f32) + delta

    @pl.when(half[0] == 0)
    def _():
        given_ref[:, :, :INNER] = mixed[...]
        regroup_into(first_ref.at[pl.ds(0, rows), :], first, FRAMES, tracks // UNIT)

    @pl.when(half[0] != 0)
    def _():
        put = pltpu.make_async_copy(mixed, mixed_hbm.at[:, pl.ds(tracks, tracks), :], sem_out)
        put.start()
        regroup_into(given_ref.reshape(rows, width), first, FRAMES, tracks // UNIT)
        put.wait()


def time_section(half, x, w_own, w_sent, back_own, back_sent):
    rows, width = x.shape
    tracks = rows // FRAMES
    vmem = pl.BlockSpec(memory_space=pltpu.VMEM)
    hbm = pl.BlockSpec(memory_space=pl.ANY)
    return pl.pallas_call(
        time_kernel,
        out_shape=[
            pltpu.VMEM((2 * rows, width), bf16),
            jax.ShapeDtypeStruct((FRAMES, 2 * tracks, INNER), bf16),
            pltpu.VMEM((FRAMES, tracks, width), bf16),
        ],
        in_specs=[
            pl.BlockSpec(memory_space=pltpu.SMEM),
            vmem,
            pl.BlockSpec(memory_space=pltpu.HBM),
            hbm,
            pl.BlockSpec(memory_space=pltpu.HBM),
            hbm,
        ],
        out_specs=[vmem, hbm, vmem],
        scratch_shapes=[
            pltpu.VMEM((width, 3 * INNER), bf16),
            pltpu.VMEM((INNER, width), bf16),
            pltpu.VMEM((FRAMES, tracks, INNER), bf16),
            pltpu.SemaphoreType.DMA,
            pltpu.SemaphoreType.DMA((3 * PAIRS,)),
            pltpu.SemaphoreType.DMA,
        ],
        compiler_params=pltpu.CompilerParams(vmem_limit_bytes=20 << 20),
        name="time_section",
    )(half, x, w_own, w_sent, back_own, back_sent)


def join_kernel(half, part_ref, first_in, mixed_in, first_out, mixed_out, sem):
    del first_in, mixed_in
    frames, tracks, width = part_ref.shape
    rows = frames * tracks

    @pl.when(half[0] == 0)
    def _():
        first_out[rows:, :] = part_ref[...].reshape(rows, width)

    @pl.when(half[0] != 0)
    def _():
        put = pltpu.make_async_copy(
            part_ref.at[:, :, pl.ds(0, INNER)], mixed_out.at[:, pl.ds(0, tracks), :], sem
        )
        put.start()
        put.wait()


def join(half, part, first, mixed):
    vmem = pl.BlockSpec(memory_space=pltpu.VMEM)
    hbm = pl.BlockSpec(memory_space=pl.ANY)
    return pl.pallas_call(
        join_kernel,
        out_shape=[
            pltpu.VMEM(first.shape, first.dtype),
            jax.ShapeDtypeStruct(mixed.shape, mixed.dtype),
        ],
        in_specs=[pl.BlockSpec(memory_space=pltpu.SMEM), vmem, vmem, hbm],
        out_specs=[vmem, hbm],
        scratch_shapes=[pltpu.SemaphoreType.DMA],
        input_output_aliases={2: 0, 3: 1},
        compiler_params=pltpu.CompilerParams(vmem_limit_bytes=4 << 20),
        name="join",
    )(half, part, first, mixed)


def track_kernel(
    planes, lists, m_ref, seen_ref, x_hbm, w0_hbm, wq_hbm, w1_hbm, o_ref,
    x_buf, w0, wq, w1, mixed0, first, qkv_0, qkv_1, qkv_2, mixed1, sem_more,
):
    rows = x_buf.shape[0]
    blocks = rows // BLOCK
    get_w0 = pltpu.make_async_copy(w0_hbm, w0, sem_more.at[0])
    get_x = pltpu.make_async_copy(x_hbm, x_buf, sem_more.at[1])
    get_w1 = pltpu.make_async_copy(w1_hbm, w1, sem_more.at[2])
    get_wq = pltpu.make_async_copy(wq_hbm, wq, sem_more.at[3])
    for copy in (get_w0, get_x, get_wq, get_w1):
        copy.start()
    regroup_into(mixed0, m_ref[...].astype(f32), FRAMES, planes)
    get_w0.wait()
    delta = jnp.dot(mixed0[...], w0[...], preferred_element_type=f32)
    get_x.wait()
    first[...] = (x_buf[...].astype(f32) + delta).astype(bf16)
    factor = row_factor(first[...])
    itself = lax.broadcasted_iota(jnp.int32, (BLOCK, BLOCK), 0) == lax.broadcasted_iota(
        jnp.int32, (BLOCK, BLOCK), 1
    )
    get_wq.wait()
    for pair, qkv in enumerate((qkv_0, qkv_1, qkv_2)):
        for part in range(3):
            at = part * INNER + pair * PAIR
            y = jnp.dot(first[...], wq[:, at : at + PAIR], preferred_element_type=f32) * factor
            qkv[:, part * PAIR : (part + 1) * PAIR] = y.astype(bf16)
        for head in range(2):
            at = head * HDIM
            out_at = (pair * 2 + head) * HDIM
            groups = []
            for block in range(blocks):
                others = [lists[block * 2], lists[block * 2 + 1]]
                places = [pl.ds(block * BLOCK, BLOCK)] + [
                    pl.ds(pl.multiple_of(o * BLOCK, BLOCK), BLOCK) for o in others
                ]
                allowed = [(seen_ref[block : block + 1, :] == 1) | itself] + [
                    seen_ref[pl.ds(o, 1), :] == 1 for o in others
                ]
                q = qkv[pl.ds(block * BLOCK, BLOCK), at : at + HDIM]
                groups.append((q, places, allowed))
            scores = [
                [
                    jnp.where(allow, similar(q, qkv[place, PAIR + at : PAIR + at + HDIM]), LOW)
                    for place, allow in zip(places, allowed)
                ]
                for q, places, allowed in groups
            ]
            tops = [
                jnp.max(functools.reduce(jnp.maximum, ss), axis=-1, keepdims=True) for ss in scores
            ]
            es = [[jnp.exp2((s - top) * SCALE) for s in ss] for ss, top in zip(scores, tops)]
            totals = [jnp.sum(sum(e[1:], e[0]), axis=-1, keepdims=True) for e in es]
            sums = [
                sum(
                    jnp.dot(
                        e.astype(bf16),
                        qkv[place, 2 * PAIR + at : 2 * PAIR + at + HDIM],
                        preferred_element_type=f32,
                    )
                    for e, place in zip(parts, places)
                )
                for parts, (q, places, allowed) in zip(es, groups)
            ]
            for block, (total, mixed) in enumerate(zip(totals, sums)):
                mixed1[block * BLOCK : (block + 1) * BLOCK, out_at : out_at + HDIM] = (
                    mixed * (1.0 / total)
                ).astype(bf16)
    get_w1.wait()
    delta = jnp.dot(mixed1[...], w1[...], preferred_element_type=f32)
    o_ref[...] = (first[...].astype(f32) + delta).astype(bf16)


def track_section(lists, x, mixed0, seen, w_out0, w_qkv, w_out1, planes):
    rows, width = x.shape
    vmem = pl.BlockSpec(memory_space=pltpu.VMEM)
    return pl.pallas_call(
        functools.partial(track_kernel, planes),
        out_shape=jax.ShapeDtypeStruct((rows, width), bf16),
        in_specs=[pl.BlockSpec(memory_space=pltpu.SMEM), vmem, vmem]
        + [pl.BlockSpec(memory_space=pltpu.HBM)] * 4,
        out_specs=vmem,
        scratch_shapes=[
            pltpu.VMEM((rows, width), bf16),
            pltpu.VMEM((INNER, width), bf16),
            pltpu.VMEM((width, 3 * INNER), bf16),
            pltpu.VMEM((INNER, width), bf16),
            pltpu.VMEM((rows, INNER), bf16),
            pltpu.VMEM((rows, width), bf16),
            pltpu.VMEM((rows, 3 * PAIR), bf16),
            pltpu.VMEM((rows, 3 * PAIR), bf16),
            pltpu.VMEM((rows, 3 * PAIR), bf16),
            pltpu.VMEM((rows, INNER), bf16),
            pltpu.SemaphoreType.DMA((4,)),
        ],
        compiler_params=pltpu.CompilerParams(vmem_limit_bytes=40 << 20),
        name="track_section",
    )(lists, mixed0, seen, x, w_out0, w_qkv, w_out1)


def exchange(value, axis):
    return lax.all_to_all(value, axis, split_axis=0, concat_axis=0, tiled=True)


def on_device(tracks_in, w_qkv, w_out, visible, neighbours):
    segment_no = lax.axis_index("segment")
    video_no = lax.axis_index("z")
    planes = lax.axis_size("z")
    frames = lax.axis_size("plane")
    x = tracks_in[0, 0]
    rows, width = x.shape
    per_chip = rows // frames
    w_in, w_back = w_qkv[0], w_out[0]
    seen = visible[0, 0].reshape(rows // BLOCK, BLOCK)
    lists = lax.dynamic_index_in_dim(neighbours[0], video_no, 0, keepdims=False).reshape(-1)
    half = segment_no.reshape(1).astype(jnp.int32)
    sent = spread(x, half, planes).reshape(frames, per_chip // 2, width)
    sent, w_in_sent, w_back_sent = lax.optimization_barrier((sent, w_in, w_back))
    moved = exchange(sent, "plane").reshape(rows // 2, width)
    w_in_first = lax.ppermute(w_in_sent, "segment", [(0, 1)])
    w_back_first = lax.ppermute(w_back_sent, "segment", [(0, 1)])
    first, mixed0, given = time_section(half, moved, w_in, w_in_first, w_back, w_back_first)
    taken = lax.ppermute(given, "segment", [(0, 1), (1, 0)])
    first, mixed0 = join(half, taken, first, mixed0)

    def track_order():
        return exchange(first.reshape(planes, -1, width), "z").reshape(rows, width)

    def section_two():
        back = exchange(mixed0, "plane").reshape(rows, INNER)
        return track_section(lists, x, back, seen, w_back_first, w_in, w_back, planes)

    result = lax.cond(segment_no == 0, track_order, section_two)
    return result[None, None, None]


def solution(mesh):
    frames = FRAMES
    devices = mesh.devices.reshape(mesh.devices.shape[0], -1, frames)
    grid = Mesh(devices, ("segment", "z", "plane"))
    seq = ("z", "plane")
    return jax.shard_map(
        on_device,
        mesh=grid,
        in_specs=(
            P(None, seq, None, None),
            P("segment", None, None),
            P("segment", None, None),
            P(None, seq, None),
            P(),
        ),
        out_specs=P("segment", None, seq, None, None),
        check_vma=False,
    )
```

```python
import functools
import math

import jax
import jax.numpy as jnp
from jax import lax
from jax.experimental import pallas as pl
from jax.experimental.pallas import tpu as pltpu
from jax.sharding import Mesh, PartitionSpec as P

HEADS = 6
HDIM = 128
BLOCK = 128
FRAMES = 16
UNIT = 4
INNER = HEADS * HDIM
PAIR = 2 * HDIM
PAIRS = HEADS // 2
EPS = 1e-06
SCALE = math.log2(math.e) / math.sqrt(HDIM)
LOW = -1e30

f32 = jnp.float32
bf16 = jnp.bfloat16


def regroup(value, outer, inner, store):
    width = value.shape[-1]
    grouped = value.reshape(outer // 2, 2, inner // 2, 8, width)
    low = lax.broadcasted_iota(jnp.int32, (8, width), 0) < 4
    for a in range(inner // 2):
        evens = [grouped[c, 0, a] for c in range(outer // 2)]
        odds = [grouped[c, 1, a] for c in range(outer // 2)]
        lower = [jnp.where(low, e, pltpu.roll(o, 4, 0)) for e, o in zip(evens, odds)]
        upper = [jnp.where(low, pltpu.roll(e, 4, 0), o) for e, o in zip(evens, odds)]
        store(a * 2 * outer * 4, jnp.concatenate(lower + upper, axis=0))


def regroup_into(o_ref, value, outer, inner):
    def store(at, rows):
        o_ref[at : at + rows.shape[0], :] = rows.astype(o_ref.dtype)

    regroup(value, outer, inner, store)


def spread_kernel(planes, half, x_hbm, o_ref, x_buf, sem):
    outer, each, width = x_buf.shape
    pieces = sem.shape[0]
    step = each // pieces
    gets = []
    for piece in range(pieces):
        part = pl.ds(piece * step, step)
        gets.append(
            pltpu.make_async_copy(
                x_hbm.at[pl.ds(half[0] * outer, outer), part, :], x_buf.at[:, part, :], sem.at[piece]
            )
        )
    for get in gets:
        get.start()
    for piece, get in enumerate(gets):
        get.wait()
        value = x_buf[:, piece * step : (piece + 1) * step, :].astype(f32)
        regroup_into(
            o_ref.at[pl.ds(piece * outer * step, outer * step), :],
            value.reshape(outer * step, width),
            outer,
            step // UNIT,
        )


def spread(x, half, planes, pieces=4):
    rows, width = x.shape
    each = rows // planes
    return pl.pallas_call(
        functools.partial(spread_kernel, planes),
        out_shape=pltpu.VMEM((rows // 2, width), bf16),
        in_specs=[pl.BlockSpec(memory_space=pltpu.SMEM), pl.BlockSpec(memory_space=pl.ANY)],
        out_specs=pl.BlockSpec(memory_space=pltpu.VMEM),
        scratch_shapes=[
            pltpu.VMEM((planes // 2, each, width), bf16),
            pltpu.SemaphoreType.DMA((pieces,)),
        ],
        compiler_params=pltpu.CompilerParams(vmem_limit_bytes=8 << 20),
        name="spread",
    )(half, x.reshape(planes, each, width))


def row_factor(x):
    wide = x.astype(f32)
    return lax.rsqrt(jnp.mean(wide * wide, axis=-1, keepdims=True) + EPS)


def similar(q, k):
    return lax.dot_general(q, k, (((1,), (1,)), ((), ())), preferred_element_type=f32)


def qkv_copies(source, target, sem):
    copies = []
    for pair in range(PAIRS):
        for part in range(3):
            columns = pl.ds(part * INNER + pair * PAIR, PAIR)
            copies.append(
                pltpu.make_async_copy(
                    source.at[:, columns], target.at[:, columns], sem.at[pair * 3 + part]
                )
            )
    return copies


def time_kernel(
    half, x_buf, own_hbm, sent_hbm, back_own, back_sent, first_ref, mixed_hbm, given_ref,
    w, w_back, mixed, sem, sem_w, sem_out,
):
    rows, width = x_buf.shape
    tracks = rows // FRAMES
    groups = tracks // 8
    side = FRAMES * 8
    get_back = pltpu.make_async_copy(back_own, w_back, sem)

    @pl.when(half[0] == 0)
    def _():
        for get in qkv_copies(own_hbm, w, sem_w):
            get.start()
        get_back.start()

    @pl.when(half[0] != 0)
    def _():
        for get in qkv_copies(sent_hbm, w, sem_w):
            get.start()
        pltpu.make_async_copy(back_sent, w_back, sem).start()

    same = (
        lax.broadcasted_iota(jnp.int32, (side, side), 0) % 8
        == lax.broadcasted_iota(jnp.int32, (side, side), 1) % 8
    )
    x = x_buf[...]
    factor = row_factor(x)
    get_w = qkv_copies(own_hbm, w, sem_w)
    for pair in range(PAIRS):
        parts = []
        for get in get_w[pair * 3 : pair * 3 + 3]:
            get.wait()
        for part in range(3):
            at = part * INNER + pair * PAIR
            y = jnp.dot(x, w[:, at : at + PAIR], preferred_element_type=f32) * factor
            parts.append(y.reshape(FRAMES, tracks, PAIR))
        places = [(head, group) for head in range(2) for group in range(groups)]
        blocks = [
            [
                y[:, group * 8 : group * 8 + 8, head * HDIM : head * HDIM + HDIM]
                .reshape(side, HDIM)
                .astype(bf16)
                for y in parts
            ]
            for head, group in places
        ]
        scores = [jnp.where(same, similar(q, k), LOW) for q, k, v in blocks]
        tops = [jnp.max(s, axis=-1, keepdims=True) for s in scores]
        es = [jnp.exp2((s - top) * SCALE) for s, top in zip(scores, tops)]
        totals = [jnp.sum(e, axis=-1, keepdims=True) for e in es]
        sums = [
            jnp.dot(e.astype(bf16), v, preferred_element_type=f32) for e, (q, k, v) in zip(es, blocks)
        ]
        for (head, group), total, summed in zip(places, totals, sums):
            at = (pair * 2 + head) * HDIM
            mixed[:, group * 8 : group * 8 + 8, at : at + HDIM] = (
                (summed * (1.0 / total)).reshape(FRAMES, 8, HDIM).astype(bf16)
            )
    m = mixed[...].reshape(rows, INNER)
    get_back.wait()
    delta = jnp.dot(m, w_back[...], preferred_element_type=f32)
    first = x.astype(f32) + delta

    @pl.when(half[0] == 0)
    def _():
        given_ref[:, :, :INNER] = mixed[...]
        regroup_into(first_ref.at[pl.ds(0, rows), :], first, FRAMES, tracks // UNIT)

    @pl.when(half[0] != 0)
    def _():
        put = pltpu.make_async_copy(mixed, mixed_hbm.at[:, pl.ds(tracks, tracks), :], sem_out)
        put.start()
        regroup_into(given_ref.reshape(rows, width), first, FRAMES, tracks // UNIT)
        put.wait()


def time_section(half, x, w_own, w_sent, back_own, back_sent):
    rows, width = x.shape
    tracks = rows // FRAMES
    vmem = pl.BlockSpec(memory_space=pltpu.VMEM)
    hbm = pl.BlockSpec(memory_space=pl.ANY)
    return pl.pallas_call(
        time_kernel,
        out_shape=[
            pltpu.VMEM((2 * rows, width), bf16),
            jax.ShapeDtypeStruct((FRAMES, 2 * tracks, INNER), bf16),
            pltpu.VMEM((FRAMES, tracks, width), bf16),
        ],
        in_specs=[
            pl.BlockSpec(memory_space=pltpu.SMEM),
            vmem,
            pl.BlockSpec(memory_space=pltpu.HBM),
            hbm,
            pl.BlockSpec(memory_space=pltpu.HBM),
            hbm,
        ],
        out_specs=[vmem, hbm, vmem],
        scratch_shapes=[
            pltpu.VMEM((width, 3 * INNER), bf16),
            pltpu.VMEM((INNER, width), bf16),
            pltpu.VMEM((FRAMES, tracks, INNER), bf16),
            pltpu.SemaphoreType.DMA,
            pltpu.SemaphoreType.DMA((3 * PAIRS,)),
            pltpu.SemaphoreType.DMA,
        ],
        compiler_params=pltpu.CompilerParams(vmem_limit_bytes=20 << 20),
        name="time_section",
    )(half, x, w_own, w_sent, back_own, back_sent)


def join_kernel(half, part_ref, first_in, mixed_in, first_out, mixed_out, sem):
    del first_in, mixed_in
    frames, tracks, width = part_ref.shape
    rows = frames * tracks

    @pl.when(half[0] == 0)
    def _():
        first_out[rows:, :] = part_ref[...].reshape(rows, width)

    @pl.when(half[0] != 0)
    def _():
        put = pltpu.make_async_copy(
            part_ref.at[:, :, pl.ds(0, INNER)], mixed_out.at[:, pl.ds(0, tracks), :], sem
        )
        put.start()
        put.wait()


def join(half, part, first, mixed):
    vmem = pl.BlockSpec(memory_space=pltpu.VMEM)
    hbm = pl.BlockSpec(memory_space=pl.ANY)
    return pl.pallas_call(
        join_kernel,
        out_shape=[
            pltpu.VMEM(first.shape, first.dtype),
            jax.ShapeDtypeStruct(mixed.shape, mixed.dtype),
        ],
        in_specs=[pl.BlockSpec(memory_space=pltpu.SMEM), vmem, vmem, hbm],
        out_specs=[vmem, hbm],
        scratch_shapes=[pltpu.SemaphoreType.DMA],
        input_output_aliases={2: 0, 3: 1},
        compiler_params=pltpu.CompilerParams(vmem_limit_bytes=4 << 20),
        name="join",
    )(half, part, first, mixed)


def track_kernel(
    planes, lists, m_ref, seen_ref, x_hbm, w0_hbm, wq_hbm, w1_hbm, o_ref,
    x_buf, w0, wq, w1, mixed0, first, qkv_0, qkv_1, qkv_2, mixed1, sem_more,
):
    rows = x_buf.shape[0]
    blocks = rows // BLOCK
    get_w0 = pltpu.make_async_copy(w0_hbm, w0, sem_more.at[0])
    get_x = pltpu.make_async_copy(x_hbm, x_buf, sem_more.at[1])
    get_w1 = pltpu.make_async_copy(w1_hbm, w1, sem_more.at[2])
    get_wq = pltpu.make_async_copy(wq_hbm, wq, sem_more.at[3])
    for copy in (get_w0, get_x, get_wq, get_w1):
        copy.start()
    regroup_into(mixed0, m_ref[...].astype(f32), FRAMES, planes)
    get_w0.wait()
    delta = jnp.dot(mixed0[...], w0[...], preferred_element_type=f32)
    get_x.wait()
    first[...] = (x_buf[...].astype(f32) + delta).astype(bf16)
    factor = row_factor(first[...])
    itself = lax.broadcasted_iota(jnp.int32, (BLOCK, BLOCK), 0) == lax.broadcasted_iota(
        jnp.int32, (BLOCK, BLOCK), 1
    )
    get_wq.wait()
    for pair, qkv in enumerate((qkv_0, qkv_1, qkv_2)):
        for part in range(3):
            at = part * INNER + pair * PAIR
            y = jnp.dot(first[...], wq[:, at : at + PAIR], preferred_element_type=f32) * factor
            qkv[:, part * PAIR : (part + 1) * PAIR] = y.astype(bf16)
        for head in range(2):
            at = head * HDIM
            out_at = (pair * 2 + head) * HDIM
            groups = []
            for block in range(blocks):
                others = [lists[block * 2], lists[block * 2 + 1]]
                places = [pl.ds(block * BLOCK, BLOCK)] + [
                    pl.ds(pl.multiple_of(o * BLOCK, BLOCK), BLOCK) for o in others
                ]
                allowed = [(seen_ref[block : block + 1, :] == 1) | itself] + [
                    seen_ref[pl.ds(o, 1), :] == 1 for o in others
                ]
                q = qkv[pl.ds(block * BLOCK, BLOCK), at : at + HDIM]
                groups.append((q, places, allowed))
            scores = [
                [
                    jnp.where(allow, similar(q, qkv[place, PAIR + at : PAIR + at + HDIM]), LOW)
                    for place, allow in zip(places, allowed)
                ]
                for q, places, allowed in groups
            ]
            tops = [
                jnp.max(functools.reduce(jnp.maximum, ss), axis=-1, keepdims=True) for ss in scores
            ]
            es = [[jnp.exp2((s - top) * SCALE) for s in ss] for ss, top in zip(scores, tops)]
            totals = [jnp.sum(sum(e[1:], e[0]), axis=-1, keepdims=True) for e in es]
            sums = [
                sum(
                    jnp.dot(
                        e.astype(bf16),
                        qkv[place, 2 * PAIR + at : 2 * PAIR + at + HDIM],
                        preferred_element_type=f32,
                    )
                    for e, place in zip(parts, places)
                )
                for parts, (q, places, allowed) in zip(es, groups)
            ]
            for block, (total, mixed) in enumerate(zip(totals, sums)):
                mixed1[block * BLOCK : (block + 1) * BLOCK, out_at : out_at + HDIM] = (
                    mixed * (1.0 / total)
                ).astype(bf16)
    get_w1.wait()
    delta = jnp.dot(mixed1[...], w1[...], preferred_element_type=f32)
    o_ref[...] = (first[...].astype(f32) + delta).astype(bf16)


def track_section(lists, x, mixed0, seen, w_out0, w_qkv, w_out1, planes):
    rows, width = x.shape
    vmem = pl.BlockSpec(memory_space=pltpu.VMEM)
    return pl.pallas_call(
        functools.partial(track_kernel, planes),
        out_shape=jax.ShapeDtypeStruct((rows, width), bf16),
        in_specs=[pl.BlockSpec(memory_space=pltpu.SMEM), vmem, vmem]
        + [pl.BlockSpec(memory_space=pltpu.HBM)] * 4,
        out_specs=vmem,
        scratch_shapes=[
            pltpu.VMEM((rows, width), bf16),
            pltpu.VMEM((INNER, width), bf16),
            pltpu.VMEM((width, 3 * INNER), bf16),
            pltpu.VMEM((INNER, width), bf16),
            pltpu.VMEM((rows, INNER), bf16),
            pltpu.VMEM((rows, width), bf16),
            pltpu.VMEM((rows, 3 * PAIR), bf16),
            pltpu.VMEM((rows, 3 * PAIR), bf16),
            pltpu.VMEM((rows, 3 * PAIR), bf16),
            pltpu.VMEM((rows, INNER), bf16),
            pltpu.SemaphoreType.DMA((4,)),
        ],
        compiler_params=pltpu.CompilerParams(vmem_limit_bytes=40 << 20),
        name="track_section",
    )(lists, mixed0, seen, x, w_out0, w_qkv, w_out1)


def exchange(value, axis):
    return lax.all_to_all(value, axis, split_axis=0, concat_axis=0, tiled=True)


def on_device(tracks_in, w_qkv, w_out, visible, neighbours):
    segment_no = lax.axis_index("segment")
    video_no = lax.axis_index("z")
    planes = lax.axis_size("z")
    frames = lax.axis_size("plane")
    x = tracks_in[0, 0]
    rows, width = x.shape
    per_chip = rows // frames
    w_in, w_back = w_qkv[0], w_out[0]
    seen = visible[0, 0].reshape(rows // BLOCK, BLOCK)
    lists = lax.dynamic_index_in_dim(neighbours[0], video_no, 0, keepdims=False).reshape(-1)
    half = segment_no.reshape(1).astype(jnp.int32)
    sent = spread(x, half, planes).reshape(frames, per_chip // 2, width)
    sent, w_in_sent, w_back_sent = lax.optimization_barrier((sent, w_in, w_back))
    moved = exchange(sent, "plane").reshape(rows // 2, width)
    w_in_first = lax.ppermute(w_in_sent, "segment", [(0, 1)])
    w_back_first = lax.ppermute(w_back_sent, "segment", [(0, 1)])
    first, mixed0, given = time_section(half, moved, w_in, w_in_first, w_back, w_back_first)
    taken = lax.ppermute(given, "segment", [(0, 1), (1, 0)])
    first, mixed0 = join(half, taken, first, mixed0)

    def track_order():
        return exchange(first.reshape(planes, -1, width), "z").reshape(rows, width)

    def section_two():
        back = exchange(mixed0, "plane").reshape(rows, INNER)
        return track_section(lists, x, back, seen, w_back_first, w_in, w_back, planes)

    result = lax.cond(segment_no == 0, track_order, section_two)
    return result[None, None, None]


def solution(mesh):
    frames = FRAMES
    devices = mesh.devices.reshape(mesh.devices.shape[0], -1, frames)
    grid = Mesh(devices, ("segment", "z", "plane"))
    seq = ("z", "plane")
    return jax.shard_map(
        on_device,
        mesh=grid,
        in_specs=(
            P(None, seq, None, None),
            P("segment", None, None),
            P("segment", None, None),
            P(None, seq, None),
            P(),
        ),
        out_specs=P("segment", None, seq, None, None),
        check_vma=False,
    )
```

```python
import functools
import math

import jax
import jax.numpy as jnp
from jax import lax
from jax.experimental import pallas as pl
from jax.experimental.pallas import tpu as pltpu
from jax.sharding import Mesh, PartitionSpec as P

HEADS = 6
HDIM = 128
BLOCK = 128
FRAMES = 16
UNIT = 4
INNER = HEADS * HDIM
PAIR = 2 * HDIM
PAIRS = HEADS // 2
EPS = 1e-06
SCALE = math.log2(math.e) / math.sqrt(HDIM)
LOW = -1e30

f32 = jnp.float32
bf16 = jnp.bfloat16


def regroup(value, outer, inner, store):
    width = value.shape[-1]
    grouped = value.reshape(outer // 2, 2, inner // 2, 8, width)
    low = lax.broadcasted_iota(jnp.int32, (8, width), 0) < 4
    for a in range(inner // 2):
        evens = [grouped[c, 0, a] for c in range(outer // 2)]
        odds = [grouped[c, 1, a] for c in range(outer // 2)]
        lower = [jnp.where(low, e, pltpu.roll(o, 4, 0)) for e, o in zip(evens, odds)]
        upper = [jnp.where(low, pltpu.roll(e, 4, 0), o) for e, o in zip(evens, odds)]
        store(a * 2 * outer * 4, jnp.concatenate(lower + upper, axis=0))


def regroup_into(o_ref, value, outer, inner):
    def store(at, rows):
        o_ref[at : at + rows.shape[0], :] = rows.astype(o_ref.dtype)

    regroup(value, outer, inner, store)


def spread_kernel(planes, half, x_hbm, o_ref, x_buf, sem):
    outer, each, width = x_buf.shape
    pieces = sem.shape[0]
    step = each // pieces
    gets = []
    for piece in range(pieces):
        part = pl.ds(piece * step, step)
        gets.append(
            pltpu.make_async_copy(
                x_hbm.at[pl.ds(half[0] * outer, outer), part, :], x_buf.at[:, part, :], sem.at[piece]
            )
        )
    for get in gets:
        get.start()
    for piece, get in enumerate(gets):
        get.wait()
        value = x_buf[:, piece * step : (piece + 1) * step, :].astype(f32)
        regroup_into(
            o_ref.at[pl.ds(piece * outer * step, outer * step), :],
            value.reshape(outer * step, width),
            outer,
            step // UNIT,
        )


def spread(x, half, planes, pieces=4):
    rows, width = x.shape
    each = rows // planes
    return pl.pallas_call(
        functools.partial(spread_kernel, planes),
        out_shape=pltpu.VMEM((rows // 2, width), bf16),
        in_specs=[pl.BlockSpec(memory_space=pltpu.SMEM), pl.BlockSpec(memory_space=pl.ANY)],
        out_specs=pl.BlockSpec(memory_space=pltpu.VMEM),
        scratch_shapes=[
            pltpu.VMEM((planes // 2, each, width), bf16),
            pltpu.SemaphoreType.DMA((pieces,)),
        ],
        compiler_params=pltpu.CompilerParams(vmem_limit_bytes=8 << 20),
        name="spread",
    )(half, x.reshape(planes, each, width))


def row_factor(x):
    wide = x.astype(f32)
    return lax.rsqrt(jnp.mean(wide * wide, axis=-1, keepdims=True) + EPS)


def similar(q, k):
    return lax.dot_general(q, k, (((1,), (1,)), ((), ())), preferred_element_type=f32)


def qkv_copies(source, target, sem):
    copies = []
    for pair in range(PAIRS):
        for part in range(3):
            columns = pl.ds(part * INNER + pair * PAIR, PAIR)
            copies.append(
                pltpu.make_async_copy(
                    source.at[:, columns], target.at[:, columns], sem.at[pair * 3 + part]
                )
            )
    return copies


def time_kernel(
    half, x_buf, own_hbm, sent_hbm, back_own, back_sent, first_ref, mixed_hbm, given_ref,
    w, w_back, mixed, sem, sem_w, sem_out,
):
    rows, width = x_buf.shape
    tracks = rows // FRAMES
    groups = tracks // 8
    side = FRAMES * 8
    get_back = pltpu.make_async_copy(back_own, w_back, sem)

    @pl.when(half[0] == 0)
    def _():
        for get in qkv_copies(own_hbm, w, sem_w):
            get.start()
        get_back.start()

    @pl.when(half[0] != 0)
    def _():
        for get in qkv_copies(sent_hbm, w, sem_w):
            get.start()
        pltpu.make_async_copy(back_sent, w_back, sem).start()

    same = (
        lax.broadcasted_iota(jnp.int32, (side, side), 0) % 8
        == lax.broadcasted_iota(jnp.int32, (side, side), 1) % 8
    )
    x = x_buf[...]
    factor = row_factor(x)
    get_w = qkv_copies(own_hbm, w, sem_w)
    for pair in range(PAIRS):
        parts = []
        for get in get_w[pair * 3 : pair * 3 + 3] if pair else ():
            get.wait()
        for part in range(3):
            if pair == 0:
                get_w[part].wait()
            at = part * INNER + pair * PAIR
            y = jnp.dot(x, w[:, at : at + PAIR], preferred_element_type=f32) * factor
            parts.append(y.reshape(FRAMES, tracks, PAIR))
        places = [(head, group) for head in range(2) for group in range(groups)]
        blocks = [
            [
                y[:, group * 8 : group * 8 + 8, head * HDIM : head * HDIM + HDIM]
                .reshape(side, HDIM)
                .astype(bf16)
                for y in parts
            ]
            for head, group in places
        ]
        scores = [jnp.where(same, similar(q, k), LOW) for q, k, v in blocks]
        tops = [jnp.max(s, axis=-1, keepdims=True) for s in scores]
        es = [jnp.exp2((s - top) * SCALE) for s, top in zip(scores, tops)]
        totals = [jnp.sum(e, axis=-1, keepdims=True) for e in es]
        sums = [
            jnp.dot(e.astype(bf16), v, preferred_element_type=f32) for e, (q, k, v) in zip(es, blocks)
        ]
        for (head, group), total, summed in zip(places, totals, sums):
            at = (pair * 2 + head) * HDIM
            mixed[:, group * 8 : group * 8 + 8, at : at + HDIM] = (
                (summed * (1.0 / total)).reshape(FRAMES, 8, HDIM).astype(bf16)
            )
    m = mixed[...].reshape(rows, INNER)
    get_back.wait()
    delta = jnp.dot(m, w_back[...], preferred_element_type=f32)
    first = x.astype(f32) + delta

    @pl.when(half[0] == 0)
    def _():
        given_ref[:, :, :INNER] = mixed[...]
        regroup_into(first_ref.at[pl.ds(0, rows), :], first, FRAMES, tracks // UNIT)

    @pl.when(half[0] != 0)
    def _():
        put = pltpu.make_async_copy(mixed, mixed_hbm.at[:, pl.ds(tracks, tracks), :], sem_out)
        put.start()
        regroup_into(given_ref.reshape(rows, width), first, FRAMES, tracks // UNIT)
        put.wait()


def time_section(half, x, w_own, w_sent, back_own, back_sent):
    rows, width = x.shape
    tracks = rows // FRAMES
    vmem = pl.BlockSpec(memory_space=pltpu.VMEM)
    hbm = pl.BlockSpec(memory_space=pl.ANY)
    return pl.pallas_call(
        time_kernel,
        out_shape=[
            pltpu.VMEM((2 * rows, width), bf16),
            jax.ShapeDtypeStruct((FRAMES, 2 * tracks, INNER), bf16),
            pltpu.VMEM((FRAMES, tracks, width), bf16),
        ],
        in_specs=[
            pl.BlockSpec(memory_space=pltpu.SMEM),
            vmem,
            pl.BlockSpec(memory_space=pltpu.HBM),
            hbm,
            pl.BlockSpec(memory_space=pltpu.HBM),
            hbm,
        ],
        out_specs=[vmem, hbm, vmem],
        scratch_shapes=[
            pltpu.VMEM((width, 3 * INNER), bf16),
            pltpu.VMEM((INNER, width), bf16),
            pltpu.VMEM((FRAMES, tracks, INNER), bf16),
            pltpu.SemaphoreType.DMA,
            pltpu.SemaphoreType.DMA((3 * PAIRS,)),
            pltpu.SemaphoreType.DMA,
        ],
        compiler_params=pltpu.CompilerParams(vmem_limit_bytes=20 << 20),
        name="time_section",
    )(half, x, w_own, w_sent, back_own, back_sent)


def join_kernel(half, part_ref, first_in, mixed_in, first_out, mixed_out, sem):
    del first_in, mixed_in
    frames, tracks, width = part_ref.shape
    rows = frames * tracks

    @pl.when(half[0] == 0)
    def _():
        first_out[rows:, :] = part_ref[...].reshape(rows, width)

    @pl.when(half[0] != 0)
    def _():
        put = pltpu.make_async_copy(
            part_ref.at[:, :, pl.ds(0, INNER)], mixed_out.at[:, pl.ds(0, tracks), :], sem
        )
        put.start()
        put.wait()


def join(half, part, first, mixed):
    vmem = pl.BlockSpec(memory_space=pltpu.VMEM)
    hbm = pl.BlockSpec(memory_space=pl.ANY)
    return pl.pallas_call(
        join_kernel,
        out_shape=[
            pltpu.VMEM(first.shape, first.dtype),
            jax.ShapeDtypeStruct(mixed.shape, mixed.dtype),
        ],
        in_specs=[pl.BlockSpec(memory_space=pltpu.SMEM), vmem, vmem, hbm],
        out_specs=[vmem, hbm],
        scratch_shapes=[pltpu.SemaphoreType.DMA],
        input_output_aliases={2: 0, 3: 1},
        compiler_params=pltpu.CompilerParams(vmem_limit_bytes=4 << 20),
        name="join",
    )(half, part, first, mixed)


def track_kernel(
    planes, lists, m_ref, seen_ref, x_hbm, w0_hbm, wq_hbm, w1_hbm, o_ref,
    x_buf, w0, wq, w1, mixed0, first, qkv_0, qkv_1, qkv_2, mixed1, bias, sem_more,
):
    rows = x_buf.shape[0]
    blocks = rows // BLOCK
    get_w0 = pltpu.make_async_copy(w0_hbm, w0, sem_more.at[0])
    get_x = pltpu.make_async_copy(x_hbm, x_buf, sem_more.at[1])
    get_w1 = pltpu.make_async_copy(w1_hbm, w1, sem_more.at[2])
    get_wq = pltpu.make_async_copy(wq_hbm, wq, sem_more.at[3])
    for copy in (get_w0, get_x, get_wq, get_w1):
        copy.start()
    regroup_into(mixed0, m_ref[...].astype(f32), FRAMES, planes)
    get_w0.wait()
    delta = jnp.dot(mixed0[...], w0[...], preferred_element_type=f32)
    get_x.wait()
    first[...] = (x_buf[...].astype(f32) + delta).astype(bf16)
    factor = row_factor(first[...])
    itself = lax.broadcasted_iota(jnp.int32, (BLOCK, BLOCK), 0) == lax.broadcasted_iota(
        jnp.int32, (BLOCK, BLOCK), 1
    )
    for block in range(blocks):
        for other in range(blocks):
            seen = seen_ref[other : other + 1, :] == 1
            if other == block:
                penalty = jnp.where(seen | itself, 0.0, LOW)
            else:
                listed = (lists[block * 2] == other) | (lists[block * 2 + 1] == other)
                row = jnp.where(seen, jnp.where(listed, 0.0, LOW), LOW)
                penalty = jnp.broadcast_to(row, (BLOCK, BLOCK))
            at = (slice(block * BLOCK, (block + 1) * BLOCK), slice(other * BLOCK, (other + 1) * BLOCK))
            bias[at] = penalty
    get_wq.wait()
    for pair, qkv in enumerate((qkv_0, qkv_1, qkv_2)):
        for part in range(3):
            at = part * INNER + pair * PAIR
            y = jnp.dot(first[...], wq[:, at : at + PAIR], preferred_element_type=f32) * factor
            qkv[:, part * PAIR : (part + 1) * PAIR] = y.astype(bf16)
        ats = [head * HDIM for head in range(2)]
        scores = [
            similar(qkv[:, at : at + HDIM], qkv[:, PAIR + at : PAIR + at + HDIM]) + bias[...]
            for at in ats
        ]
        tops = [jnp.max(s, axis=-1, keepdims=True) for s in scores]
        es = [jnp.exp2((s - top) * SCALE) for s, top in zip(scores, tops)]
        totals = [jnp.sum(e, axis=-1, keepdims=True) for e in es]
        sums = [
            jnp.dot(
                e.astype(bf16),
                qkv[:, 2 * PAIR + at : 2 * PAIR + at + HDIM],
                preferred_element_type=f32,
            )
            for e, at in zip(es, ats)
        ]
        for at, total, summed in zip(ats, totals, sums):
            out_at = pair * PAIR + at
            mixed1[:, out_at : out_at + HDIM] = (summed * (1.0 / total)).astype(bf16)
    get_w1.wait()
    delta = jnp.dot(mixed1[...], w1[...], preferred_element_type=f32)
    o_ref[...] = (first[...].astype(f32) + delta).astype(bf16)


def track_section(lists, x, mixed0, seen, w_out0, w_qkv, w_out1, planes):
    rows, width = x.shape
    vmem = pl.BlockSpec(memory_space=pltpu.VMEM)
    return pl.pallas_call(
        functools.partial(track_kernel, planes),
        out_shape=jax.ShapeDtypeStruct((rows, width), bf16),
        in_specs=[pl.BlockSpec(memory_space=pltpu.SMEM), vmem, vmem]
        + [pl.BlockSpec(memory_space=pltpu.HBM)] * 4,
        out_specs=vmem,
        scratch_shapes=[
            pltpu.VMEM((rows, width), bf16),
            pltpu.VMEM((INNER, width), bf16),
            pltpu.VMEM((width, 3 * INNER), bf16),
            pltpu.VMEM((INNER, width), bf16),
            pltpu.VMEM((rows, INNER), bf16),
            pltpu.VMEM((rows, width), bf16),
            pltpu.VMEM((rows, 3 * PAIR), bf16),
            pltpu.VMEM((rows, 3 * PAIR), bf16),
            pltpu.VMEM((rows, 3 * PAIR), bf16),
            pltpu.VMEM((rows, INNER), bf16),
            pltpu.VMEM((rows, rows), f32),
            pltpu.SemaphoreType.DMA((4,)),
        ],
        compiler_params=pltpu.CompilerParams(vmem_limit_bytes=40 << 20),
        name="track_section",
    )(lists, mixed0, seen, x, w_out0, w_qkv, w_out1)


def exchange(value, axis):
    return lax.all_to_all(value, axis, split_axis=0, concat_axis=0, tiled=True)


def on_device(tracks_in, w_qkv, w_out, visible, neighbours):
    segment_no = lax.axis_index("segment")
    video_no = lax.axis_index("z")
    planes = lax.axis_size("z")
    frames = lax.axis_size("plane")
    x = tracks_in[0, 0]
    rows, width = x.shape
    per_chip = rows // frames
    w_in, w_back = w_qkv[0], w_out[0]
    seen = visible[0, 0].reshape(rows // BLOCK, BLOCK)
    lists = lax.dynamic_index_in_dim(neighbours[0], video_no, 0, keepdims=False).reshape(-1)
    half = segment_no.reshape(1).astype(jnp.int32)
    sent = spread(x, half, planes).reshape(frames, per_chip // 2, width)
    sent, w_in_sent, w_back_sent = lax.optimization_barrier((sent, w_in, w_back))
    moved = exchange(sent, "plane").reshape(rows // 2, width)
    w_in_first = lax.ppermute(w_in_sent, "segment", [(0, 1)])
    w_back_first = lax.ppermute(w_back_sent, "segment", [(0, 1)])
    first, mixed0, given = time_section(half, moved, w_in, w_in_first, w_back, w_back_first)
    taken = lax.ppermute(given, "segment", [(0, 1), (1, 0)])
    first, mixed0 = join(half, taken, first, mixed0)

    def track_order():
        return exchange(first.reshape(planes, -1, width), "z").reshape(rows, width)

    def section_two():
        back = exchange(mixed0, "plane").reshape(rows, INNER)
        return track_section(lists, x, back, seen, w_back_first, w_in, w_back, planes)

    result = lax.cond(segment_no == 0, track_order, section_two)
    return result[None, None, None]


def solution(mesh):
    frames = FRAMES
    devices = mesh.devices.reshape(mesh.devices.shape[0], -1, frames)
    grid = Mesh(devices, ("segment", "z", "plane"))
    seq = ("z", "plane")
    return jax.shard_map(
        on_device,
        mesh=grid,
        in_specs=(
            P(None, seq, None, None),
            P("segment", None, None),
            P("segment", None, None),
            P(None, seq, None),
            P(),
        ),
        out_specs=P("segment", None, seq, None, None),
        check_vma=False,
    )
```

```python
import functools
import math

import jax
import jax.numpy as jnp
from jax import lax
from jax.experimental import pallas as pl
from jax.experimental.pallas import tpu as pltpu
from jax.sharding import Mesh, PartitionSpec as P

HEADS = 6
HDIM = 128
BLOCK = 128
FRAMES = 16
UNIT = 4
INNER = HEADS * HDIM
PAIR = 2 * HDIM
PAIRS = HEADS // 2
EPS = 1e-06
SCALE = math.log2(math.e) / math.sqrt(HDIM)
LOW = -1e30

f32 = jnp.float32
bf16 = jnp.bfloat16


def regroup(value, outer, inner, store):
    width = value.shape[-1]
    grouped = value.reshape(outer // 2, 2, inner // 2, 8, width)
    low = lax.broadcasted_iota(jnp.int32, (8, width), 0) < 4
    for a in range(inner // 2):
        evens = [grouped[c, 0, a] for c in range(outer // 2)]
        odds = [grouped[c, 1, a] for c in range(outer // 2)]
        lower = [jnp.where(low, e, pltpu.roll(o, 4, 0)) for e, o in zip(evens, odds)]
        upper = [jnp.where(low, pltpu.roll(e, 4, 0), o) for e, o in zip(evens, odds)]
        store(a * 2 * outer * 4, jnp.concatenate(lower + upper, axis=0))


def regroup_into(o_ref, value, outer, inner):
    def store(at, rows):
        o_ref[at : at + rows.shape[0], :] = rows.astype(o_ref.dtype)

    regroup(value, outer, inner, store)


def spread_kernel(planes, half, x_hbm, o_ref, x_buf, sem):
    outer, each, width = x_buf.shape
    pieces = sem.shape[0]
    step = each // pieces
    gets = []
    for piece in range(pieces):
        part = pl.ds(piece * step, step)
        gets.append(
            pltpu.make_async_copy(
                x_hbm.at[pl.ds(half[0] * outer, outer), part, :], x_buf.at[:, part, :], sem.at[piece]
            )
        )
    for get in gets:
        get.start()
    for piece, get in enumerate(gets):
        get.wait()
        value = x_buf[:, piece * step : (piece + 1) * step, :].astype(f32)
        regroup_into(
            o_ref.at[pl.ds(piece * outer * step, outer * step), :],
            value.reshape(outer * step, width),
            outer,
            step // UNIT,
        )


def spread(x, half, planes, pieces=2):
    rows, width = x.shape
    each = rows // planes
    return pl.pallas_call(
        functools.partial(spread_kernel, planes),
        out_shape=pltpu.VMEM((rows // 2, width), bf16),
        in_specs=[pl.BlockSpec(memory_space=pltpu.SMEM), pl.BlockSpec(memory_space=pl.ANY)],
        out_specs=pl.BlockSpec(memory_space=pltpu.VMEM),
        scratch_shapes=[
            pltpu.VMEM((planes // 2, each, width), bf16),
            pltpu.SemaphoreType.DMA((pieces,)),
        ],
        compiler_params=pltpu.CompilerParams(vmem_limit_bytes=8 << 20),
        name="spread",
    )(half, x.reshape(planes, each, width))


def row_factor(x):
    wide = x.astype(f32)
    return lax.rsqrt(jnp.mean(wide * wide, axis=-1, keepdims=True) + EPS)


def similar(q, k):
    return lax.dot_general(q, k, (((1,), (1,)), ((), ())), preferred_element_type=f32)


def qkv_copies(source, target, sem):
    copies = []
    for pair in range(PAIRS):
        for part in range(3):
            columns = pl.ds(part * INNER + pair * PAIR, PAIR)
            copies.append(
                pltpu.make_async_copy(
                    source.at[:, columns], target.at[:, columns], sem.at[pair * 3 + part]
                )
            )
    return copies


def time_kernel(
    half, x_buf, own_hbm, sent_hbm, back_own, back_sent, first_ref, mixed_hbm, given_ref,
    w, w_back, mixed, sem, sem_w, sem_out,
):
    rows, width = x_buf.shape
    tracks = rows // FRAMES
    groups = tracks // 8
    side = FRAMES * 8
    get_back = pltpu.make_async_copy(back_own, w_back, sem)

    @pl.when(half[0] == 0)
    def _():
        for get in qkv_copies(own_hbm, w, sem_w):
            get.start()
        get_back.start()

    @pl.when(half[0] != 0)
    def _():
        for get in qkv_copies(sent_hbm, w, sem_w):
            get.start()
        pltpu.make_async_copy(back_sent, w_back, sem).start()

    same = (
        lax.broadcasted_iota(jnp.int32, (side, side), 0) % 8
        == lax.broadcasted_iota(jnp.int32, (side, side), 1) % 8
    )
    x = x_buf[...]
    factor = row_factor(x)
    get_w = qkv_copies(own_hbm, w, sem_w)
    for pair in range(PAIRS):
        parts = []
        for get in get_w[pair * 3 : pair * 3 + 3] if pair else ():
            get.wait()
        for part in range(3):
            if pair == 0:
                get_w[part].wait()
            at = part * INNER + pair * PAIR
            y = jnp.dot(x, w[:, at : at + PAIR], preferred_element_type=f32) * factor
            parts.append(y.reshape(FRAMES, tracks, PAIR))
        places = [(head, group) for head in range(2) for group in range(groups)]
        blocks = [
            [
                y[:, group * 8 : group * 8 + 8, head * HDIM : head * HDIM + HDIM]
                .reshape(side, HDIM)
                .astype(bf16)
                for y in parts
            ]
            for head, group in places
        ]
        scores = [jnp.where(same, similar(q, k), LOW) for q, k, v in blocks]
        tops = [jnp.max(s, axis=-1, keepdims=True) for s in scores]
        es = [jnp.exp2((s - top) * SCALE) for s, top in zip(scores, tops)]
        totals = [jnp.sum(e, axis=-1, keepdims=True) for e in es]
        sums = [
            jnp.dot(e.astype(bf16), v, preferred_element_type=f32) for e, (q, k, v) in zip(es, blocks)
        ]
        for (head, group), total, summed in zip(places, totals, sums):
            at = (pair * 2 + head) * HDIM
            mixed[:, group * 8 : group * 8 + 8, at : at + HDIM] = (
                (summed * (1.0 / total)).reshape(FRAMES, 8, HDIM).astype(bf16)
            )
    m = mixed[...].reshape(rows, INNER)
    get_back.wait()
    delta = jnp.dot(m, w_back[...], preferred_element_type=f32)
    first = x.astype(f32) + delta

    @pl.when(half[0] == 0)
    def _():
        given_ref[:, :, :INNER] = mixed[...]
        regroup_into(first_ref.at[pl.ds(0, rows), :], first, FRAMES, tracks // UNIT)

    @pl.when(half[0] != 0)
    def _():
        put = pltpu.make_async_copy(mixed, mixed_hbm.at[:, pl.ds(tracks, tracks), :], sem_out)
        put.start()
        regroup_into(given_ref.reshape(rows, width), first, FRAMES, tracks // UNIT)
        put.wait()


def time_section(half, x, w_own, w_sent, back_own, back_sent):
    rows, width = x.shape
    tracks = rows // FRAMES
    vmem = pl.BlockSpec(memory_space=pltpu.VMEM)
    hbm = pl.BlockSpec(memory_space=pl.ANY)
    return pl.pallas_call(
        time_kernel,
        out_shape=[
            pltpu.VMEM((2 * rows, width), bf16),
            jax.ShapeDtypeStruct((FRAMES, 2 * tracks, INNER), bf16),
            pltpu.VMEM((FRAMES, tracks, width), bf16),
        ],
        in_specs=[
            pl.BlockSpec(memory_space=pltpu.SMEM),
            vmem,
            pl.BlockSpec(memory_space=pltpu.HBM),
            hbm,
            pl.BlockSpec(memory_space=pltpu.HBM),
            hbm,
        ],
        out_specs=[vmem, hbm, vmem],
        scratch_shapes=[
            pltpu.VMEM((width, 3 * INNER), bf16),
            pltpu.VMEM((INNER, width), bf16),
            pltpu.VMEM((FRAMES, tracks, INNER), bf16),
            pltpu.SemaphoreType.DMA,
            pltpu.SemaphoreType.DMA((3 * PAIRS,)),
            pltpu.SemaphoreType.DMA,
        ],
        compiler_params=pltpu.CompilerParams(vmem_limit_bytes=20 << 20),
        name="time_section",
    )(half, x, w_own, w_sent, back_own, back_sent)


def join_kernel(half, part_ref, first_in, mixed_in, first_out, mixed_out, sem):
    del first_in, mixed_in
    frames, tracks, width = part_ref.shape
    rows = frames * tracks

    @pl.when(half[0] == 0)
    def _():
        first_out[rows:, :] = part_ref[...].reshape(rows, width)

    @pl.when(half[0] != 0)
    def _():
        put = pltpu.make_async_copy(
            part_ref.at[:, :, pl.ds(0, INNER)], mixed_out.at[:, pl.ds(0, tracks), :], sem
        )
        put.start()
        put.wait()


def join(half, part, first, mixed):
    vmem = pl.BlockSpec(memory_space=pltpu.VMEM)
    hbm = pl.BlockSpec(memory_space=pl.ANY)
    return pl.pallas_call(
        join_kernel,
        out_shape=[
            pltpu.VMEM(first.shape, first.dtype),
            jax.ShapeDtypeStruct(mixed.shape, mixed.dtype),
        ],
        in_specs=[pl.BlockSpec(memory_space=pltpu.SMEM), vmem, vmem, hbm],
        out_specs=[vmem, hbm],
        scratch_shapes=[pltpu.SemaphoreType.DMA],
        input_output_aliases={2: 0, 3: 1},
        compiler_params=pltpu.CompilerParams(vmem_limit_bytes=4 << 20),
        name="join",
    )(half, part, first, mixed)


def track_kernel(
    planes, lists, m_ref, seen_ref, x_hbm, w0_hbm, wq_hbm, w1_hbm, o_ref,
    x_buf, w0, wq, w1, mixed0, first, qkv_0, qkv_1, qkv_2, mixed1, bias, sem_more,
):
    rows = x_buf.shape[0]
    blocks = rows // BLOCK
    get_w0 = pltpu.make_async_copy(w0_hbm, w0, sem_more.at[0])
    get_x = pltpu.make_async_copy(x_hbm, x_buf, sem_more.at[1])
    get_w1 = pltpu.make_async_copy(w1_hbm, w1, sem_more.at[2])
    get_wq = pltpu.make_async_copy(wq_hbm, wq, sem_more.at[3])
    for copy in (get_w0, get_x, get_wq, get_w1):
        copy.start()
    regroup_into(mixed0, m_ref[...].astype(f32), FRAMES, planes)
    get_w0.wait()
    delta = jnp.dot(mixed0[...], w0[...], preferred_element_type=f32)
    get_x.wait()
    first[...] = (x_buf[...].astype(f32) + delta).astype(bf16)
    factor = row_factor(first[...])
    itself = lax.broadcasted_iota(jnp.int32, (BLOCK, BLOCK), 0) == lax.broadcasted_iota(
        jnp.int32, (BLOCK, BLOCK), 1
    )
    for block in range(blocks):
        for other in range(blocks):
            seen = seen_ref[other : other + 1, :] == 1
            if other == block:
                penalty = jnp.where(seen | itself, 0.0, LOW)
            else:
                listed = (lists[block * 2] == other) | (lists[block * 2 + 1] == other)
                row = jnp.where(seen, jnp.where(listed, 0.0, LOW), LOW)
                penalty = jnp.broadcast_to(row, (BLOCK, BLOCK))
            at = (slice(block * BLOCK, (block + 1) * BLOCK), slice(other * BLOCK, (other + 1) * BLOCK))
            bias[at] = penalty
    get_wq.wait()
    for pair, qkv in enumerate((qkv_0, qkv_1, qkv_2)):
        for part in range(3):
            at = part * INNER + pair * PAIR
            y = jnp.dot(first[...], wq[:, at : at + PAIR], preferred_element_type=f32) * factor
            qkv[:, part * PAIR : (part + 1) * PAIR] = y.astype(bf16)
        ats = [head * HDIM for head in range(2)]
        scores = [
            similar(qkv[:, at : at + HDIM], qkv[:, PAIR + at : PAIR + at + HDIM]) + bias[...]
            for at in ats
        ]
        tops = [jnp.max(s, axis=-1, keepdims=True) for s in scores]
        es = [jnp.exp2((s - top) * SCALE) for s, top in zip(scores, tops)]
        totals = [jnp.sum(e, axis=-1, keepdims=True) for e in es]
        sums = [
            jnp.dot(
                e.astype(bf16),
                qkv[:, 2 * PAIR + at : 2 * PAIR + at + HDIM],
                preferred_element_type=f32,
            )
            for e, at in zip(es, ats)
        ]
        for at, total, summed in zip(ats, totals, sums):
            out_at = pair * PAIR + at
            mixed1[:, out_at : out_at + HDIM] = (summed * (1.0 / total)).astype(bf16)
    get_w1.wait()
    delta = jnp.dot(mixed1[...], w1[...], preferred_element_type=f32)
    o_ref[...] = (first[...].astype(f32) + delta).astype(bf16)


def track_section(lists, x, mixed0, seen, w_out0, w_qkv, w_out1, planes):
    rows, width = x.shape
    vmem = pl.BlockSpec(memory_space=pltpu.VMEM)
    return pl.pallas_call(
        functools.partial(track_kernel, planes),
        out_shape=jax.ShapeDtypeStruct((rows, width), bf16),
        in_specs=[pl.BlockSpec(memory_space=pltpu.SMEM), vmem, vmem]
        + [pl.BlockSpec(memory_space=pltpu.HBM)] * 4,
        out_specs=vmem,
        scratch_shapes=[
            pltpu.VMEM((rows, width), bf16),
            pltpu.VMEM((INNER, width), bf16),
            pltpu.VMEM((width, 3 * INNER), bf16),
            pltpu.VMEM((INNER, width), bf16),
            pltpu.VMEM((rows, INNER), bf16),
            pltpu.VMEM((rows, width), bf16),
            pltpu.VMEM((rows, 3 * PAIR), bf16),
            pltpu.VMEM((rows, 3 * PAIR), bf16),
            pltpu.VMEM((rows, 3 * PAIR), bf16),
            pltpu.VMEM((rows, INNER), bf16),
            pltpu.VMEM((rows, rows), f32),
            pltpu.SemaphoreType.DMA((4,)),
        ],
        compiler_params=pltpu.CompilerParams(vmem_limit_bytes=40 << 20),
        name="track_section",
    )(lists, mixed0, seen, x, w_out0, w_qkv, w_out1)


def exchange(value, axis):
    return lax.all_to_all(value, axis, split_axis=0, concat_axis=0, tiled=True)


def on_device(tracks_in, w_qkv, w_out, visible, neighbours):
    segment_no = lax.axis_index("segment")
    video_no = lax.axis_index("z")
    planes = lax.axis_size("z")
    frames = lax.axis_size("plane")
    x = tracks_in[0, 0]
    rows, width = x.shape
    per_chip = rows // frames
    w_in, w_back = w_qkv[0], w_out[0]
    seen = visible[0, 0].reshape(rows // BLOCK, BLOCK)
    lists = lax.dynamic_index_in_dim(neighbours[0], video_no, 0, keepdims=False).reshape(-1)
    half = segment_no.reshape(1).astype(jnp.int32)
    sent = spread(x, half, planes).reshape(frames, per_chip // 2, width)
    sent, w_in_sent, w_back_sent = lax.optimization_barrier((sent, w_in, w_back))
    moved = exchange(sent, "plane").reshape(rows // 2, width)
    w_in_first = lax.ppermute(w_in_sent, "segment", [(0, 1)])
    w_back_first = lax.ppermute(w_back_sent, "segment", [(0, 1)])
    first, mixed0, given = time_section(half, moved, w_in, w_in_first, w_back, w_back_first)
    taken = lax.ppermute(given, "segment", [(0, 1), (1, 0)])
    first, mixed0 = join(half, taken, first, mixed0)

    def track_order():
        return exchange(first.reshape(planes, -1, width), "z").reshape(rows, width)

    def section_two():
        back = exchange(mixed0, "plane").reshape(rows, INNER)
        return track_section(lists, x, back, seen, w_back_first, w_in, w_back, planes)

    result = lax.cond(segment_no == 0, track_order, section_two)
    return result[None, None, None]


def solution(mesh):
    frames = FRAMES
    devices = mesh.devices.reshape(mesh.devices.shape[0], -1, frames)
    grid = Mesh(devices, ("segment", "z", "plane"))
    seq = ("z", "plane")
    return jax.shard_map(
        on_device,
        mesh=grid,
        in_specs=(
            P(None, seq, None, None),
            P("segment", None, None),
            P("segment", None, None),
            P(None, seq, None),
            P(),
        ),
        out_specs=P("segment", None, seq, None, None),
        check_vma=False,
    )
```
